32 devices in a mesh: cube: 4 (over y, x), panel: 8 (over z, core).
Axes of the slice: x: 2, y: 2, z: 4, core: 2. Of those that a mesh axis runs over, the one named last changes fastest.
Arguments:
- columns: bfloat16 [96, 4, 4096], P('cube', None, 'panel'), may hold values from -8 to 8
- leaf_of: int32 [96, 1], P('cube'), may hold values from 0 to 3; in each aligned block of 24 rows (0 to 23, 24 to 47, ...) at most 12 rows name the same one
- inverse_root: bfloat16 [4096, 4096], P('cube', 'panel'), may hold values from -0.5 to 0.5, as said below
- inverse_upper: bfloat16 [8192, 4096], P('cube', 'panel'), may hold values from -0.5 to 0.5, as said below
- inverse_middle: bfloat16 [16384, 4096], P('cube', 'panel'), may hold values from -0.5 to 0.5, as said below
- inverse_leaf: bfloat16 [16384, 4096], P('cube', 'panel'), may hold values from -0.5 to 0.5, as said below
- coupling_upper: bfloat16 [8192, 1, 4096], P('cube', None, 'panel'), may hold values from -6 to 6
- coupling_middle: bfloat16 [16384, 2, 4096], P('cube', None, 'panel'), may hold values from -6 to 6
- coupling_leaf: bfloat16 [16384, 3, 4096], P('cube', None, 'panel'), may hold values from -6 to 6
Outputs:
- core_factor: float32 [192, 192], replicated
- project_root: bfloat16 [4096, 192], P(('cube', 'panel'))
- project_upper: bfloat16 [8192, 96], P(('cube', 'panel'))
- project_middle: bfloat16 [16384, 48], P(('cube', 'panel'))
- project_leaf: bfloat16 [16384, 48], P(('cube', 'panel'))
The draws below stay inside these ranges and needn't reach their ends.
Inputs may be any that keep to these rules, and one draw needn't show every extreme that they name: `leaf_of`: among the 24 columns held by one index of cube, no leaf is named more than 12 times. `inverse_root`: each block of 4096 rows is lower triangular. `inverse_upper`: each block of 4096 rows is lower triangular. `inverse_middle`: each block of 4096 rows is lower triangular. `inverse_leaf`: each block of 4096 rows is lower triangular.
All inputs are finite; a program needn't handle non-finite values.
Results may differ from the reference program's by a relative error of at most 0.011.
Values may be sent and summed in bfloat16 or wider, within the bound.
A program may use at most 128 MiB of HBM per device.

```python
import math
import jax
import jax.numpy as jnp
import numpy as np

NS = 4096
TIME_DEV = 24
RANK = 96
LEAVES = 4
MIDDLE_NODES = 4
UPPER_NODES = 2
LEAF_SPAN = 1
M = 12
PER_SLOT = 12
C_DEV = 48
FRONT = 192
N_CUBE = 4


def draw_columns(key, part):
    key_noise, key_common, key_weight = jax.random.split(key, 3)
    noise = jnp.clip(jax.random.normal(key_noise, (RANK, 4, NS), jnp.float32), -5.0, 5.0)
    common = jnp.clip(jax.random.normal(key_common, (4, NS), jnp.float32), -5.0, 5.0)
    weights = jax.random.uniform(key_weight, (RANK,), jnp.float32, -1.0, 1.0)
    values = 0.8 * noise + 0.6 * weights[:, None, None] * common[None]
    return values.astype(jnp.bfloat16)


def lower_blocks(key, nodes, label):
    key_spread, key_diag = jax.random.split(jax.random.fold_in(key, label))
    row_pos = jnp.arange(nodes * NS, dtype=jnp.int32)[:, None] % NS
    col_pos = jnp.arange(NS, dtype=jnp.int32)[None, :]
    spread = jnp.clip(jax.random.normal(key_spread, (nodes * NS, NS), jnp.float32), -5.0, 5.0)
    diagonal = jnp.exp(jax.random.uniform(key_diag, (nodes * NS, 1), jnp.float32, math.log(0.5), math.log(2.0)))
    values = jnp.where(col_pos < row_pos, spread / NS, jnp.where(col_pos == row_pos, diagonal / math.sqrt(NS), 0.0))
    return values.astype(jnp.bfloat16)


def draw_inverse_root(key, part):
    return lower_blocks(key, 1, 11)


def draw_inverse_upper(key, part):
    return lower_blocks(key, UPPER_NODES, 13)


def draw_inverse_middle(key, part):
    return lower_blocks(key, MIDDLE_NODES, 17)


def draw_inverse_leaf(key, part):
    return lower_blocks(key, LEAVES, 19)


def block_levels(own_key, dims, cuts, smallest, high):
    def one(axis_at, blocks):
        draws = jax.random.uniform(jax.random.fold_in(jax.random.fold_in(own_key, 6), axis_at), (blocks,), jnp.float32, smallest / len(cuts), high / len(cuts))
        return jnp.repeat(jnp.exp(draws), dims[axis_at] // blocks).reshape((-1,) + (1,) * (len(dims) - axis_at - 1))

    gain = one(*cuts[0])
    for cut in cuts[1:]:
        gain = gain * one(*cut)
    return gain


def deal_out(key, own, number, rows, number_of, top, reach, skew):
    sequence = jax.random.permutation(key, number_of)
    packed, usual = portions_of(number_of, rows * top, reach, skew, True), portions_of(number_of, rows * top, reach, skew, False)
    places = jnp.arange(number_of)

    def named(lengths, turn):
        used = int((lengths > 0).sum())
        fixed = max(1, used // 4)
        passed = fixed + (places - fixed + turn * (used - fixed)) % max(1, number_of - fixed)
        return jnp.zeros((number_of,), jnp.int32).at[sequence[jnp.where(places < fixed, places, passed)]].set(jnp.asarray(lengths, jnp.int32))

    lengths = jnp.where(number % 4 == 0, named(packed, number // 4), named(usual, number - number // 4 - 1))
    mixed = jax.random.permutation(jax.random.fold_in(own, 3), number_of)
    donor, sink = mixed[0:number_of // 2 * 2:2], mixed[1:number_of // 2 * 2:2]
    margin = jnp.minimum(lengths[donor] - 1, reach - lengths[sink]) // 2
    margin = jnp.where((donor == sequence[0]) | (sink == sequence[0]) | (lengths[sink] == 0), 0, jnp.maximum(margin, 0))
    passed = jax.random.randint(jax.random.fold_in(own, 4), (number_of // 2,), 0, 1 << 20) % (margin + 1)
    lengths = lengths.at[donor].add(-passed).at[sink].add(passed)
    items = jnp.searchsorted(jnp.cumsum(lengths), jnp.arange(rows * top), side="right").astype(jnp.int32)
    listing = items.reshape(top, rows).T
    listing = listing[jax.random.permutation(jax.random.fold_in(own, 1), rows)]
    turn = jax.random.randint(jax.random.fold_in(own, 2), (rows, 1), 0, top)
    return jnp.take_along_axis(listing, (jnp.arange(top)[None, :] + turn) % top, axis=1)


def portions_of(count, total, limit, slope, full):
    loads = [(1 << 20) // math.isqrt(standing ** slope) + 1 for standing in range(1, count + 1)]
    largest = limit if full else min(limit, max(-(-total // count), total * loads[0] // sum(loads)))
    least = 1 if total - largest >= count - 1 else 0
    given, spare = [largest] + [least] * (count - 1), total - largest - least * (count - 1)
    while spare > 0:
        free = [i for i in range(1, count) if given[i] < largest] or [i for i in range(1, count) if given[i] < limit]
        whole, budget = sum([loads[i] for i in free]), spare
        for i in free:
            more = min(limit - given[i], max(1, budget * loads[i] // whole), spare)
            given[i] = given[i] + more
            spare = spare - more
    return np.array(given)


def normal_values(stream_key, shape, scale, most, cuts=(), kind=jnp.bfloat16):
    loudness = block_levels(stream_key, shape, cuts, -0.22, 0.18) if cuts else 1.0
    array = jax.random.normal(stream_key, shape, jnp.float32) * scale * loudness
    return jnp.minimum(jnp.maximum(array, -most), most).astype(kind)


def setup_inputs(seed: int = 0) -> dict:
    splits = jax.random.split(jax.random.key(seed), 10)
    columns = draw_columns(jax.random.fold_in(splits[9], 71), 0)
    leaf_of_keys = jax.random.split(jax.random.fold_in(splits[1], 1), RANK // TIME_DEV)
    leaf_of_turns = jax.random.permutation(jax.random.fold_in(splits[1], 3), RANK // TIME_DEV)
    leaf_of = jax.vmap(lambda own, number: deal_out(jax.random.fold_in(splits[1], 2), own, number, TIME_DEV, LEAVES, 1, M, 2))(leaf_of_keys, leaf_of_turns).reshape((RANK, 1))
    inverse_root = draw_inverse_root(jax.random.fold_in(splits[9], 71), 0)
    inverse_upper = draw_inverse_upper(jax.random.fold_in(splits[9], 71), 0)
    inverse_middle = draw_inverse_middle(jax.random.fold_in(splits[9], 71), 0)
    inverse_leaf = draw_inverse_leaf(jax.random.fold_in(splits[9], 71), 0)
    coupling_upper = normal_values(splits[6], (UPPER_NODES * NS, 1, NS), 1.0, 6.0, ((0, 4), (2, 8)))
    coupling_middle = normal_values(splits[7], (MIDDLE_NODES * NS, 2, NS), 1.0, 6.0, ((0, 4), (2, 8)))
    coupling_leaf = normal_values(splits[8], (LEAVES * NS, 3, NS), 1.0, 6.0, ((0, 4), (2, 8)))
    return dict(columns=columns, leaf_of=leaf_of, inverse_root=inverse_root, inverse_upper=inverse_upper, inverse_middle=inverse_middle, inverse_leaf=inverse_leaf, coupling_upper=coupling_upper, coupling_middle=coupling_middle, coupling_leaf=coupling_leaf)


def route_front(columns, leaf_of):
    labels = leaf_of[:, 0].reshape(N_CUBE, TIME_DEV)
    onehot = (labels[:, :, None] == jnp.arange(LEAVES, dtype=jnp.int32)[None, None, :]).astype(jnp.int32)
    before = jnp.cumsum(onehot, axis=1, dtype=jnp.int32) - onehot
    within = jnp.sum(before * onehot, axis=2, dtype=jnp.int32)
    sender = jnp.arange(N_CUBE, dtype=jnp.int32)[:, None]
    destination = (labels * LEAF_SPAN + within // PER_SLOT) * C_DEV + sender * PER_SLOT + within % PER_SLOT
    empty = jnp.zeros((FRONT, 4, NS), jnp.bfloat16)
    return empty.at[destination.reshape(-1).astype(jnp.int32)].set(columns)

def reference(columns, leaf_of, inverse_root, inverse_upper, inverse_middle, inverse_leaf, coupling_upper, coupling_middle, coupling_leaf):
    front_cols = route_front(columns, leaf_of)
    inverses = (inverse_root, inverse_upper, inverse_middle, inverse_leaf)
    couplings = (None, coupling_upper, coupling_middle, coupling_leaf)
    results = [None, None, None, None]
    factor = None
    for tree_level in (3, 2, 1, 0):
        node_count = min(2 ** tree_level, N_CUBE)
        group_width = FRONT // node_count
        pieces = []
        fronts = []
        for node in range(node_count):
            block_cols = front_cols[node * group_width:(node + 1) * group_width]
            inverse = inverses[tree_level][node * NS:(node + 1) * NS]
            projected = jnp.dot(inverse.astype(jnp.float32), block_cols[:, 0, :].T.astype(jnp.float32), preferred_element_type=jnp.float32).astype(jnp.bfloat16)
            gram_local = jnp.dot(projected.T.astype(jnp.float32), projected.astype(jnp.float32), preferred_element_type=jnp.float32)
            factor = jnp.linalg.cholesky(jnp.eye(group_width, dtype=jnp.float32) + gram_local)
            pieces.append(projected)
            if tree_level > 0:
                coupling = couplings[tree_level][node * NS:(node + 1) * NS].reshape(NS, tree_level * NS)
                cross_term = jnp.dot(projected.T.astype(jnp.float32), coupling.astype(jnp.float32), preferred_element_type=jnp.float32)
                remainder = block_cols[:, 1:, :].reshape(group_width, tree_level * NS).astype(jnp.float32) - cross_term
                solved = jax.scipy.linalg.solve_triangular(factor, remainder, lower=True)
                fronts.append(solved.astype(jnp.bfloat16).reshape(group_width, tree_level, NS))
        results[tree_level] = jnp.concatenate(pieces, 0)
        if tree_level > 0:
            front_cols = jnp.concatenate(fronts, 0)
    return (factor, results[0], results[1], results[2], results[3])
```

```python
import functools

import jax
import jax.numpy as jnp
from jax import lax
from jax.experimental import pallas as pl
from jax.experimental.pallas import tpu as pltpu
from jax.sharding import PartitionSpec as P

MESH = pl.DeviceIdType.MESH
LEVELS = (3, 2, 1, 0)
SLOT = 16
NT = (((1,), (1,)), ((), ()))
NN = (((1,), (0,)), ((), ()))
TN = (((0,), (0,)), ((), ()))


def radices(size):
    steps = []
    while size > 1:
        steps.append(min(4, size))
        size //= steps[-1]
    return steps


def mm(a, b, dims):
    return lax.dot_general(a, b, dims, preferred_element_type=jnp.float32)


def mm32(a, b, dims):
    return lax.dot_general(
        a, b, dims, precision=lax.Precision.HIGHEST, preferred_element_type=jnp.float32
    )


def factor_block(block, work):
    n = block.shape[0]
    work[:, :n] = block
    row_pos = lax.broadcasted_iota(jnp.int32, (n, 128), 0)
    lane_pos = lax.broadcasted_iota(jnp.int32, (n, 128), 1)
    m = jnp.where(lane_pos < n, work[...], 0.0) + (lane_pos == row_pos + 64).astype(jnp.float32)
    done = []
    for j in range(0, n, 2):
        if j and j % 8 == 0:
            done.append(m[:8])
            m = m[8:]
        at = j % 8
        shape = m.shape
        here = row_pos[: shape[0]]
        first = jnp.broadcast_to(m[:, j : j + 1], shape)
        second = jnp.broadcast_to(m[:, j + 1 : j + 2], shape)
        a, b, d = first[at : at + 1], first[at + 1 : at + 2], second[at + 1 : at + 2]
        over_a, over_d = 1.0 / a, a * (1.0 / (a * d - b * b))
        ratio = b * over_a
        top, next_row = m[at : at + 1], m[at + 1 : at + 2]
        low = jnp.where(here > at + 1, second - ratio * first, 0.0)
        first = jnp.where(here > at, first, 0.0)
        m = m - first * (top * over_a) - low * ((next_row - ratio * top) * over_d)
    m = jnp.concatenate(done + [m], axis=0)
    pivots = jnp.sum(jnp.where(lane_pos == row_pos, m, 0.0), axis=1, keepdims=True)
    m = m * lax.rsqrt(pivots)
    upper = jnp.where(lane_pos >= row_pos, m, 0.0)[:, :n]
    return upper, m[:, 64 : 64 + n]


def eye(n):
    return (
        lax.broadcasted_iota(jnp.int32, (n, n), 0) == lax.broadcasted_iota(jnp.int32, (n, n), 1)
    ).astype(jnp.float32)


def factor_panels(total, width, work):
    count = total.shape[0] // width
    panels = [total[k * width :, k * width : (k + 1) * width] for k in range(count)]
    result = []
    for k in range(count):
        upper, inverse = factor_block(panels[k][:width], work)
        below = None
        if k + 1 < count:
            below = mm32(panels[k][width:], inverse, NT)
            for j in range(k + 1, count):
                at = (j - k - 1) * width
                panels[j] = panels[j] - mm32(below[at:], below[at : at + width], NT)
        result.append((upper, inverse, below))
    return result


def kernel(cube, panel, width, per_slot, leaves, geometry, *refs):
    refs = list(refs)
    take = lambda count: [refs.pop(0) for _ in range(count)]
    labels, columns = take(2)
    inv_hbm = dict(zip(LEVELS, take(4)))
    coup_hbm = dict(zip(LEVELS[:3], take(3)))
    core_out = take(1)[0]
    proj_out = dict(zip(LEVELS, take(4)))
    inv = dict(zip(LEVELS, take(4)))
    coup = dict(zip(LEVELS[:3], take(3)))
    packed, arrived, place, places = take(4)
    front = dict(zip(LEVELS, take(4)))
    twin_sent = dict(zip(LEVELS, take(4)))
    twin_got = dict(zip(LEVELS, take(4)))
    sent = dict(zip(LEVELS, take(4)))
    got = dict(zip(LEVELS, take(4)))
    full = dict(zip(LEVELS, take(4)))
    gram = dict(zip(LEVELS, take(4)))
    gram_part = dict(zip(LEVELS, take(4)))
    cross = dict(zip(LEVELS[:3], take(3)))
    cross_part = dict(zip(LEVELS[:3], take(3)))
    solved = dict(zip(LEVELS[:3], take(3)))
    work, low_factor = take(2)
    load_sem, route_send, route_recv, place_send, place_recv, panel_send, panel_recv, cube_send, cube_recv = take(9)

    c = lax.axis_index("cube")
    p = lax.axis_index("panel")
    chips = panel // 2
    chip, core = lax.div(p, 2), lax.rem(p, 2)

    loads = {}
    for at, level in enumerate(LEVELS):
        loads[level] = [pltpu.make_async_copy(inv_hbm[level], inv[level], load_sem.at[at, 0])]
        if level:
            loads[level].append(
                pltpu.make_async_copy(coup_hbm[level], coup[level], load_sem.at[at, 1])
            )
    loads[LEVELS[0]][0].start()

    barrier = pltpu.get_barrier_semaphore()

    def greet(axis, me, size):
        def one(d, carry):
            pl.semaphore_signal(
                barrier, inc=1, device_id={axis: lax.rem(me + d, size)}, device_id_type=MESH
            )
            return carry

        lax.fori_loop(1, size, one, 0)

    greet("cube", c, cube)
    greet("panel", p, panel)

    def greet_across(d, carry):
        pl.semaphore_signal(
            barrier, inc=1, device_id=(lax.rem(c + d, cube), p + 1 - 2 * core), device_id_type=MESH
        )
        return carry

    lax.fori_loop(1, cube, greet_across, 0)

    label = labels[...]
    time_cols = label.shape[1]
    share = cube // leaves
    onehot = lax.broadcasted_iota(jnp.int32, (16, time_cols), 0) == label
    earlier = lax.broadcasted_iota(jnp.int32, (time_cols, time_cols), 0) < (
        lax.broadcasted_iota(jnp.int32, (time_cols, time_cols), 1)
    )
    onehot = onehot.astype(jnp.float32)
    before = mm(onehot.astype(jnp.bfloat16), earlier.astype(jnp.float32).astype(jnp.bfloat16), NN)
    within = jnp.sum(before * onehot, axis=0, keepdims=True).astype(jnp.int32)
    turn = jnp.zeros_like(within)
    for step in range(1, share):
        turn = turn + (within >= step * per_slot).astype(jnp.int32)
    target = (label * share + turn) * SLOT + within - turn * per_slot
    slot = (label * share + turn) * width + c * per_slot + within - turn * per_slot
    place[...] = jnp.zeros(place.shape, jnp.int32)
    place[:1, :time_cols] = slot
    dispatch = (
        (lax.broadcasted_iota(jnp.int32, (cube * SLOT, time_cols), 0) == target)
        .astype(jnp.float32)
        .astype(jnp.bfloat16)
    )
    for j in range(4):
        block = mm(dispatch, columns[j], NN).astype(jnp.bfloat16)
        packed[:, j] = block.reshape(cube, SLOT, block.shape[1])

    pl.semaphore_wait(barrier, 2 * cube + panel - 3)
    for level in LEVELS:
        for load in loads[level]:
            if load is not loads[LEVELS[0]][0]:
                load.start()

    def route(d):
        to = lax.rem(c + d, cube)
        return pltpu.make_async_remote_copy(
            src_ref=packed.at[to],
            dst_ref=arrived.at[c],
            send_sem=route_send.at[d],
            recv_sem=route_recv.at[d],
            device_id={"cube": to},
            device_id_type=MESH,
        )

    def each(low, high, do):
        def one(d, carry):
            do(d)
            return carry

        lax.fori_loop(low, high, one, 0)

    def tell(d):
        return pltpu.make_async_remote_copy(
            src_ref=place,
            dst_ref=places.at[c],
            send_sem=place_send.at[d],
            recv_sem=place_recv.at[d],
            device_id={"cube": lax.rem(c + d, cube)},
            device_id_type=MESH,
        )

    each(1, cube, lambda d: route(d).start())
    each(1, cube, lambda d: tell(d).start())
    arrived[c] = packed[c]
    places[c] = place[...]
    each(1, cube, lambda d: route(d).wait_recv())
    out_pos = lax.broadcasted_iota(jnp.int32, (width, cube * SLOT), 0)
    in_pos = lax.broadcasted_iota(jnp.int32, (width, cube * SLOT), 1)
    select = jnp.zeros((width, cube * SLOT), jnp.float32)
    for s in range(cube):
        hit = (in_pos - s * SLOT == out_pos - s * per_slot) & (out_pos >= s * per_slot)
        hit = hit & (out_pos < (s + 1) * per_slot)
        select = select + hit.astype(jnp.float32)
    select = select.astype(jnp.bfloat16)
    first_size, _ = geometry[3][:2]
    first_rank = lax.rem(c, first_size)
    for j in range(4):
        mine = mm(select, arrived[:, j].reshape(cube * SLOT, arrived.shape[3]), NN)
        front[3][first_rank, j] = mine.astype(jnp.bfloat16)

    pending = []

    def compact():
        each(1, cube, lambda d: tell(d).wait_recv())
        wide = cube * width
        slot_pos = lax.broadcasted_iota(jnp.int32, (wide, time_cols), 0)
        ones = jnp.ones((8, time_cols), jnp.bfloat16)
        used = jnp.zeros((8, wide), jnp.float32)
        for s in range(cube):
            at_slot = (slot_pos == places[s, :1, :time_cols]).astype(jnp.float32)
            used = used + mm(ones, at_slot.astype(jnp.bfloat16), NT)
        ahead = lax.broadcasted_iota(jnp.int32, (wide, wide), 0) < (
            lax.broadcasted_iota(jnp.int32, (wide, wide), 1)
        )
        count = mm(used.astype(jnp.bfloat16), ahead.astype(jnp.float32).astype(jnp.bfloat16), NN)
        row = lax.broadcasted_iota(jnp.int32, (cube * time_cols, wide), 0)
        hit = (row == count[:1].astype(jnp.int32)) & (used[:1] > 0.5)
        return hit.astype(jnp.float32)

    def settle(copy, radix):
        each(1, radix, lambda d: copy(d).wait_recv())

    def fold(slots, stage, radix):
        value = slots[stage, 0].astype(jnp.float32)
        for s in range(1, radix):
            value = value + slots[stage, s].astype(jnp.float32)
        return value

    def group_copy(level, phase, src, dst, size, d):
        rank = lax.rem(c, size)
        to = c - rank + lax.rem(rank + d, size)
        return pltpu.make_async_remote_copy(
            src_ref=src,
            dst_ref=dst,
            send_sem=cube_send.at[level, phase, d],
            recv_sem=cube_recv.at[level, phase, d],
            device_id={"cube": to},
            device_id_type=MESH,
        )

    def share_front(level, size, source):
        rank = lax.rem(c, size)
        if source is not None:
            front[level][rank] = source
        if size > 1:
            copy = lambda d: group_copy(
                level, 0, front[level].at[rank], front[level].at[rank], size, d
            )
            each(1, size, lambda d: copy(d).start())
            each(1, size, lambda d: copy(d).wait_recv())
            pending.append((1, size, copy))

    share_front(3, first_size, None)

    for at, level in enumerate(LEVELS):
        size, rows, part = geometry[level]
        wide = size * width
        rank = lax.rem(c, size)
        stripe = front[level].shape[3]
        top = front[level][:, 0].reshape(wide, stripe)
        if not level:
            pick = compact()
            top = mm(pick.astype(jnp.bfloat16), top, NN).astype(jnp.bfloat16)
            wide = top.shape[0]
        loads[level][0].wait()

        def term(z, core, level=level, part=part, top=top):
            at_row = pl.multiple_of((2 * z + core) * part, part)
            return mm(top, inv[level][pl.ds(at_row, part), :], NT)

        def panel_copy(kind, src, dst, d, z, core, level=level):
            return pltpu.make_async_remote_copy(
                src_ref=src,
                dst_ref=dst,
                send_sem=panel_send.at[level, kind, d],
                recv_sem=panel_recv.at[level, kind, d],
                device_id={"panel": 2 * z + core},
                device_id_type=MESH,
            )

        def to_twin(d, level=level, panel_copy=panel_copy):
            return panel_copy(0, twin_sent[level].at[d], twin_got[level].at[d], d, chip, 1 - core)

        def scatter(d, level=level, panel_copy=panel_copy):
            to = lax.rem(chip + d, chips)
            return panel_copy(1, sent[level].at[d], got[level].at[d], d, to, 1 - core)

        def send_twin(d, side, level=level, term=term, to_twin=to_twin):
            twin_sent[level][d] = term(lax.rem(chip + d, chips), side).astype(jnp.bfloat16)
            to_twin(d).start()

        def send_term(d, level=level, term=term, to_twin=to_twin, scatter=scatter):
            mine = term(lax.rem(chip + d, chips), 1 - core)
            to_twin(d).wait_recv()
            sent[level][d] = (mine + twin_got[level][d].astype(jnp.float32)).astype(jnp.bfloat16)
            scatter(d).start()

        each(1, chips, lambda d, send_twin=send_twin: send_twin(d, core))
        send_twin(0, 1 - core)
        each(1, chips, send_term)
        own = term(chip, core)
        to_twin(0).wait_recv()
        own = own + twin_got[level][0].astype(jnp.float32)
        for d in range(1, chips):
            scatter(d).wait_recv()
            own = own + got[level][d].astype(jnp.float32)
        own = own.astype(jnp.bfloat16)
        full[level][chip, core] = own

        def gather(d, level=level, panel_copy=panel_copy):
            here = full[level].at[chip, core]
            return panel_copy(2, here, here, d, lax.rem(chip + d, chips), 1 - core)

        def forward(d, side, level=level, panel_copy=panel_copy):
            here = full[level].at[lax.rem(chip + chips - d, chips), side]
            return panel_copy(3, here, here, d, chip, 1 - core)

        each(1, chips, lambda d, gather=gather: gather(d).start())
        forward(0, core).start()
        if level:
            proj_out[level][...] = own
        else:
            proj_out[level][...] = mm(pick.astype(jnp.bfloat16), own, TN).astype(jnp.bfloat16)
        pending.append((0, chips, to_twin))
        pending.append((1, chips, scatter))
        pending.append((1, chips, gather))
        pending.append((0, 1, lambda d, forward=forward: forward(d, core)))
        pending.append((1, chips, lambda d, forward=forward: forward(d, 1 - core)))

        if level:
            loads[level][1].wait()

        def add_chunk(z, core, first, level=level, part=part):
            chunk = full[level][z, core]
            value = mm(chunk, chunk, NT)
            gram[level][...] = value if first else gram[level][...] + value
            for j in range(level):
                at_row = pl.multiple_of((2 * z + core) * part, part)
                value = mm(chunk, coup[level][j, pl.ds(at_row, part), :], NN)
                cross[level][j] = value if first else cross[level][j] + value

        add_chunk(chip, core, True)

        def receive(d, gather=gather, forward=forward, add_chunk=add_chunk):
            gather(d).wait_recv()
            forward(d, 1 - core).start()
            add_chunk(lax.rem(chip + chips - d, chips), 1 - core, False)

        def receive_twin(d, side, forward=forward, add_chunk=add_chunk):
            forward(d, 1 - side).wait_recv()
            add_chunk(lax.rem(chip + chips - d, chips), side, False)

        receive_twin(0, 1 - core)
        each(1, chips, receive)
        each(1, chips, lambda d, receive_twin=receive_twin: receive_twin(d, core))

        steps = radices(size)
        stride = 1
        copies = None
        for stage, radix in enumerate(steps):
            if stage and level:
                settle(copies[1], radix_before)
                cross[level][...] = fold(cross_part[level], stage - 1, radix_before)
            digit = lax.rem(lax.div(rank, stride), radix)
            copies = []
            for kind, slots, acc in ((0, gram_part, gram), (1, cross_part, cross)):
                if kind and not level:
                    continue
                slots[level][stage, digit] = acc[level][...].astype(slots[level].dtype)

                def copy(d, kind=kind, slot=slots[level], stage=stage, digit=digit, stride=stride, radix=radix, level=level):
                    return pltpu.make_async_remote_copy(
                        src_ref=slot.at[stage, digit],
                        dst_ref=slot.at[stage, digit],
                        send_sem=cube_send.at[level, 1 + 2 * stage + kind, d],
                        recv_sem=cube_recv.at[level, 1 + 2 * stage + kind, d],
                        device_id=(
                            c + (lax.rem(digit + d, radix) - digit) * stride,
                            p if kind else p + 1 - 2 * core,
                        ),
                        device_id_type=MESH,
                    )

                each(1, radix, lambda d, copy=copy: copy(d).start())
                pending.append((1, radix, copy))
                copies.append(copy)
            settle(copies[0], radix)
            gram[level][...] = fold(gram_part[level], stage, radix)
            radix_before, stride = radix, stride * radix
        total = eye(wide) + gram[level][...]
        blocks = factor_panels(total, width, work)
        if not level:
            low_factor[...] = jnp.zeros(low_factor.shape, jnp.float32)
            for k, (upper, _, below) in enumerate(blocks):
                low = k * width
                low_factor[low : low + width, low : low + width] = mm32(eye(width), upper, NT)
                if below is not None:
                    low_factor[low + width :, low : low + width] = below
            spread = mm32(low_factor[...], pick, NN)
            ones = jnp.ones((wide, size * width), jnp.bfloat16)
            used = mm(pick.astype(jnp.bfloat16), ones, TN)
            unused = eye(size * width) * (1.0 - used)
            core_out[...] = mm32(pick, spread, TN) + unused
            break
        if steps:
            settle(copies[1], radix_before)
            summed_all = fold(cross_part[level], len(steps) - 1, radix_before)
        for j in range(level):
            summed = summed_all[j] if steps else cross[level][j]
            for k, (_, inverse, below) in enumerate(blocks):
                low = k * width
                right = front[level][k, j + 1].astype(jnp.float32) - summed[low : low + width]
                for earlier_k in range(k):
                    at_row = (k - earlier_k - 1) * width
                    right = right - mm32(
                        blocks[earlier_k][2][at_row : at_row + width], values[earlier_k], NN
                    )
                values = [] if k == 0 else values
                values.append(mm32(inverse, right, NN))
                solved[level][k, j] = values[k].astype(jnp.bfloat16)
        share_front(level - 1, geometry[level - 1][0], solved[level][rank])

    each(1, cube, lambda d: route(d).wait_send())
    each(1, cube, lambda d: tell(d).wait_send())
    for low, high, copy in pending:
        each(low, high, lambda d, copy=copy: copy(d).wait_send())


def hand_out(*refs):
    for source, result in zip(refs[:5], refs[5:]):
        result[...] = source[...]


def body(
    cube,
    panel,
    columns,
    leaf_of,
    inverse_root,
    inverse_upper,
    inverse_middle,
    inverse_leaf,
    coupling_upper,
    coupling_middle,
    coupling_leaf,
):
    time_cols, _, stripe = columns.shape
    leaves = min(8, cube)
    leaf_share = cube // leaves
    per_slot = max(1, (2 * time_cols // leaves + leaf_share - 1) // leaf_share)
    width = cube * per_slot
    inverses = [inverse_leaf, inverse_middle, inverse_upper, inverse_root]
    couplings = [
        jnp.transpose(x, (1, 0, 2)) for x in (coupling_leaf, coupling_middle, coupling_upper)
    ]
    geometry = {}
    for level, inverse in zip(LEVELS, inverses):
        rows = inverse.shape[0]
        geometry[level] = (cube // min(2**level, cube), rows, rows // panel)
    wide = {level: geometry[level][0] * width for level in LEVELS}
    ranks = cube * time_cols
    slots = wide[0]
    wide[0] = ranks
    part = {level: geometry[level][2] for level in LEVELS}
    size = {level: geometry[level][0] for level in LEVELS}
    vm = pltpu.VMEM
    scratch = [vm(x.shape, x.dtype) for x in inverses]
    scratch += [vm(x.shape, x.dtype) for x in couplings]
    scratch += [vm((cube, 4, SLOT, stripe), jnp.bfloat16)] * 2
    scratch += [vm((8, 128), jnp.int32), vm((cube, 8, 128), jnp.int32)]
    scratch += [vm((size[l], l + 1, width, stripe), jnp.bfloat16) for l in LEVELS]
    for _ in range(4):
        scratch += [vm((panel // 2, wide[l], part[l]), jnp.bfloat16) for l in LEVELS]
    scratch += [vm((panel // 2, 2, wide[l], part[l]), jnp.bfloat16) for l in LEVELS]
    scratch += [vm((wide[l], wide[l]), jnp.float32) for l in LEVELS]
    for l in LEVELS:
        steps = radices(size[l]) or [1]
        kind = jnp.float32 if size[l] <= 2 else jnp.bfloat16
        scratch += [vm((len(steps), max(steps), wide[l], wide[l]) if size[l] > 1 else (1, 1, 8, 128), kind)]
    scratch += [vm((l, wide[l], stripe), jnp.float32) for l in LEVELS[:3]]
    for l in LEVELS[:3]:
        steps = radices(size[l]) or [1]
        scratch += [vm((len(steps), max(steps), l, wide[l], stripe), jnp.bfloat16)]
    scratch += [vm((size[l], l, width, stripe), jnp.bfloat16) for l in LEVELS[:3]]
    scratch += [vm((width, 128), jnp.float32), vm((ranks, ranks), jnp.float32)]
    dma = pltpu.SemaphoreType.DMA
    scratch += [dma((4, 2)), dma((cube,)), dma((cube,)), dma((cube,)), dma((cube,)), dma((4, 4, panel // 2)), dma((4, 4, panel // 2))]
    scratch += [dma((4, 5, cube)), dma((4, 5, cube))]
    outs = [jax.ShapeDtypeStruct((slots, slots), jnp.float32)]
    outs += [jax.ShapeDtypeStruct((wide[l], part[l]), jnp.bfloat16) for l in LEVELS[:3]]
    outs += [jax.ShapeDtypeStruct((slots, part[0]), jnp.bfloat16)]
    in_vmem = pl.BlockSpec(memory_space=pltpu.VMEM)
    in_any = pl.BlockSpec(memory_space=pl.ANY)
    core, leaf, middle, upper, root = pl.pallas_call(
        functools.partial(kernel, cube, panel, width, per_slot, leaves, geometry),
        out_shape=outs,
        in_specs=[in_vmem, in_vmem] + [in_any] * 7,
        out_specs=[in_vmem] * 5,
        scratch_shapes=scratch,
        compiler_params=pltpu.CompilerParams(
            collective_id=0, has_side_effects=True, vmem_limit_bytes=58 * 2**20
        ),
    )(
        jnp.transpose(leaf_of),
        jnp.transpose(columns, (1, 0, 2)),
        *inverses,
        *couplings,
    )
    core, leaf, middle, upper, root = pl.pallas_call(
        hand_out,
        out_shape=outs,
        in_specs=[in_vmem] * 5,
        out_specs=[in_vmem] * 5,
    )(core, leaf, middle, upper, root)
    return (core, root.T, upper.T, middle.T, leaf.T)


def solution(mesh):
    in_specs = (
        P("cube", None, "panel"),
        P("cube", None),
        P("cube", "panel"),
        P("cube", "panel"),
        P("cube", "panel"),
        P("cube", "panel"),
        P("cube", None, "panel"),
        P("cube", None, "panel"),
        P("cube", None, "panel"),
    )
    out_specs = (
        P(),
        P(("cube", "panel"), None),
        P(("cube", "panel"), None),
        P(("cube", "panel"), None),
        P(("cube", "panel"), None),
    )
    run = functools.partial(body, mesh.shape["cube"], mesh.shape["panel"])
    return jax.shard_map(run, mesh=mesh, in_specs=in_specs, out_specs=out_specs, check_vma=False)
```

```python
import functools

import jax
import jax.numpy as jnp
from jax import lax
from jax.experimental import pallas as pl
from jax.experimental.pallas import tpu as pltpu
from jax.sharding import PartitionSpec as P

MESH = pl.DeviceIdType.MESH
LEVELS = (3, 2, 1, 0)
SLOT = 16
NT = (((1,), (1,)), ((), ()))
NN = (((1,), (0,)), ((), ()))
TN = (((0,), (0,)), ((), ()))


def radices(size):
    steps = []
    while size > 1:
        steps.append(min(4, size))
        size //= steps[-1]
    return steps


def mm(a, b, dims):
    return lax.dot_general(a, b, dims, preferred_element_type=jnp.float32)


def mm32(a, b, dims):
    return lax.dot_general(
        a, b, dims, precision=lax.Precision.HIGHEST, preferred_element_type=jnp.float32
    )


def factor_block(block, work):
    n = block.shape[0]
    work[:, :n] = block
    row_pos = lax.broadcasted_iota(jnp.int32, (n, 128), 0)
    lane_pos = lax.broadcasted_iota(jnp.int32, (n, 128), 1)
    m = jnp.where(lane_pos < n, work[...], 0.0) + (lane_pos == row_pos + 64).astype(jnp.float32)
    done = []
    for j in range(0, n, 2):
        if j and j % 8 == 0:
            done.append(m[:8])
            m = m[8:]
        at = j % 8
        shape = m.shape
        here = row_pos[: shape[0]]
        first = jnp.broadcast_to(m[:, j : j + 1], shape)
        second = jnp.broadcast_to(m[:, j + 1 : j + 2], shape)
        a, b, d = first[at : at + 1], first[at + 1 : at + 2], second[at + 1 : at + 2]
        over_a, over_d = 1.0 / a, a * (1.0 / (a * d - b * b))
        ratio = b * over_a
        top, next_row = m[at : at + 1], m[at + 1 : at + 2]
        low = jnp.where(here > at + 1, second - ratio * first, 0.0)
        first = jnp.where(here > at, first, 0.0)
        m = m - first * (top * over_a) - low * ((next_row - ratio * top) * over_d)
    m = jnp.concatenate(done + [m], axis=0)
    pivots = jnp.sum(jnp.where(lane_pos == row_pos, m, 0.0), axis=1, keepdims=True)
    m = m * lax.rsqrt(pivots)
    upper = jnp.where(lane_pos >= row_pos, m, 0.0)[:, :n]
    return upper, m[:, 64 : 64 + n]


def eye(n):
    return (
        lax.broadcasted_iota(jnp.int32, (n, n), 0) == lax.broadcasted_iota(jnp.int32, (n, n), 1)
    ).astype(jnp.float32)


def factor_panels(total, width, work):
    count = total.shape[0] // width
    panels = [total[k * width :, k * width : (k + 1) * width] for k in range(count)]
    result = []
    for k in range(count):
        upper, inverse = factor_block(panels[k][:width], work)
        below = None
        if k + 1 < count:
            below = mm32(panels[k][width:], inverse, NT)
            for j in range(k + 1, count):
                at = (j - k - 1) * width
                panels[j] = panels[j] - mm32(below[at:], below[at : at + width], NT)
        result.append((upper, inverse, below))
    return result


def kernel(cube, panel, width, per_slot, leaves, geometry, *refs):
    refs = list(refs)
    take = lambda count: [refs.pop(0) for _ in range(count)]
    labels, columns = take(2)
    inv_hbm = dict(zip(LEVELS, take(4)))
    coup_hbm = dict(zip(LEVELS[:3], take(3)))
    gram_out, pick_out = take(2)
    proj_out = dict(zip(LEVELS, take(4)))
    inv = dict(zip(LEVELS, take(4)))
    coup = dict(zip(LEVELS[:3], take(3)))
    packed, arrived, place, places = take(4)
    front = dict(zip(LEVELS, take(4)))
    twin_sent = dict(zip(LEVELS, take(4)))
    twin_got = dict(zip(LEVELS, take(4)))
    sent = dict(zip(LEVELS, take(4)))
    got = dict(zip(LEVELS, take(4)))
    full = dict(zip(LEVELS, take(4)))
    gram = dict(zip(LEVELS, take(4)))
    gram_part = dict(zip(LEVELS, take(4)))
    cross = dict(zip(LEVELS[:3], take(3)))
    cross_part = dict(zip(LEVELS[:3], take(3)))
    solved = dict(zip(LEVELS[:3], take(3)))
    work = take(1)[0]
    load_sem, route_send, route_recv, place_send, place_recv, panel_send, panel_recv, cube_send, cube_recv = take(9)

    c = lax.axis_index("cube")
    p = lax.axis_index("panel")
    chips = panel // 2
    chip, core = lax.div(p, 2), lax.rem(p, 2)

    loads = {}
    for at, level in enumerate(LEVELS):
        loads[level] = [pltpu.make_async_copy(inv_hbm[level], inv[level], load_sem.at[at, 0])]
        if level:
            loads[level].append(
                pltpu.make_async_copy(coup_hbm[level], coup[level], load_sem.at[at, 1])
            )
    loads[LEVELS[0]][0].start()

    barrier = pltpu.get_barrier_semaphore()

    def greet(axis, me, size):
        def one(d, carry):
            pl.semaphore_signal(
                barrier, inc=1, device_id={axis: lax.rem(me + d, size)}, device_id_type=MESH
            )
            return carry

        lax.fori_loop(1, size, one, 0)

    greet("cube", c, cube)
    greet("panel", p, panel)

    def greet_across(d, carry):
        pl.semaphore_signal(
            barrier, inc=1, device_id=(lax.rem(c + d, cube), p + 1 - 2 * core), device_id_type=MESH
        )
        return carry

    lax.fori_loop(1, cube, greet_across, 0)

    label = labels[...]
    time_cols = label.shape[1]
    share = cube // leaves
    onehot = lax.broadcasted_iota(jnp.int32, (16, time_cols), 0) == label
    earlier = lax.broadcasted_iota(jnp.int32, (time_cols, time_cols), 0) < (
        lax.broadcasted_iota(jnp.int32, (time_cols, time_cols), 1)
    )
    onehot = onehot.astype(jnp.float32)
    before = mm(onehot.astype(jnp.bfloat16), earlier.astype(jnp.float32).astype(jnp.bfloat16), NN)
    within = jnp.sum(before * onehot, axis=0, keepdims=True).astype(jnp.int32)
    turn = jnp.zeros_like(within)
    for step in range(1, share):
        turn = turn + (within >= step * per_slot).astype(jnp.int32)
    target = (label * share + turn) * (4 * SLOT) + within - turn * per_slot
    slot = (label * share + turn) * width + c * per_slot + within - turn * per_slot
    place[...] = jnp.zeros(place.shape, jnp.int32)
    place[:1, :time_cols] = slot
    stretch = (
        lax.broadcasted_iota(jnp.int32, (time_cols, 4 * time_cols), 0)
        == lax.div(lax.broadcasted_iota(jnp.int32, (time_cols, 4 * time_cols), 1), 4)
    ).astype(jnp.float32)
    sent_to = jnp.broadcast_to(target.astype(jnp.float32), (8, time_cols))
    sent_to = mm32(sent_to, stretch, NN)[:1] + 0.5
    kind_at = lax.rem(lax.broadcasted_iota(jnp.int32, (1, 4 * time_cols), 1), 4)
    sent_to = sent_to.astype(jnp.int32) + kind_at * SLOT
    dispatch = (
        (lax.broadcasted_iota(jnp.int32, (cube * 4 * SLOT, 4 * time_cols), 0) == sent_to)
        .astype(jnp.float32)
        .astype(jnp.bfloat16)
    )
    stripe = columns.shape[2]
    by_time = columns[...].reshape(4 * time_cols, stripe)
    packed[...] = mm(dispatch, by_time, NN).astype(jnp.bfloat16).reshape(cube, 4, SLOT, stripe)

    pl.semaphore_wait(barrier, 2 * cube + panel - 3)
    for level in LEVELS:
        for load in loads[level]:
            if load is not loads[LEVELS[0]][0]:
                load.start()

    def route(d, rest):
        to = lax.rem(c + d, cube)
        blocks = pl.ds(1, 3) if rest else pl.ds(0, 1)
        return pltpu.make_async_remote_copy(
            src_ref=packed.at[to, blocks],
            dst_ref=arrived.at[c, blocks],
            send_sem=route_send.at[rest, d],
            recv_sem=route_recv.at[rest, d],
            device_id={"cube": to},
            device_id_type=MESH,
        )

    def each(low, high, do):
        def one(d, carry):
            do(d)
            return carry

        lax.fori_loop(low, high, one, 0)

    def tell(d):
        return pltpu.make_async_remote_copy(
            src_ref=place,
            dst_ref=places.at[c],
            send_sem=place_send.at[d],
            recv_sem=place_recv.at[d],
            device_id={"cube": lax.rem(c + d, cube)},
            device_id_type=MESH,
        )

    each(1, cube, lambda d: route(d, 0).start())
    each(1, cube, lambda d: route(d, 1).start())
    each(1, cube, lambda d: tell(d).start())
    arrived[c] = packed[c]
    places[c] = place[...]
    each(1, cube, lambda d: route(d, 0).wait_recv())
    out_pos = lax.broadcasted_iota(jnp.int32, (width, cube * SLOT), 0)
    in_pos = lax.broadcasted_iota(jnp.int32, (width, cube * SLOT), 1)
    select = jnp.zeros((width, cube * SLOT), jnp.float32)
    for s in range(cube):
        hit = (in_pos - s * SLOT == out_pos - s * per_slot) & (out_pos >= s * per_slot)
        hit = hit & (out_pos < (s + 1) * per_slot)
        select = select + hit.astype(jnp.float32)
    select = select.astype(jnp.bfloat16)
    first_size, _ = geometry[3][:2]
    first_rank = lax.rem(c, first_size)

    def settle_block(j):
        mine = mm(select, arrived[:, j].reshape(cube * SLOT, stripe), NN)
        front[3][first_rank, j] = mine.astype(jnp.bfloat16)

    settle_block(0)
    if first_size > 1:
        each(1, cube, lambda d: route(d, 1).wait_recv())
        for j in range(1, 4):
            settle_block(j)

    pending = []

    def compact():
        each(1, cube, lambda d: tell(d).wait_recv())
        wide = cube * width
        slot_pos = lax.broadcasted_iota(jnp.int32, (wide, time_cols), 0)
        ones = jnp.ones((8, time_cols), jnp.bfloat16)
        used = jnp.zeros((8, wide), jnp.float32)
        for s in range(cube):
            at_slot = (slot_pos == places[s, :1, :time_cols]).astype(jnp.float32)
            used = used + mm(ones, at_slot.astype(jnp.bfloat16), NT)
        ahead = lax.broadcasted_iota(jnp.int32, (wide, wide), 0) < (
            lax.broadcasted_iota(jnp.int32, (wide, wide), 1)
        )
        count = mm(used.astype(jnp.bfloat16), ahead.astype(jnp.float32).astype(jnp.bfloat16), NN)
        row = lax.broadcasted_iota(jnp.int32, (cube * time_cols, wide), 0)
        hit = (row == count[:1].astype(jnp.int32)) & (used[:1] > 0.5)
        return hit.astype(jnp.float32)

    def settle(copy, radix):
        each(1, radix, lambda d: copy(d).wait_recv())

    def fold(slots, stage, radix):
        value = slots[stage, 0].astype(jnp.float32)
        for s in range(1, radix):
            value = value + slots[stage, s].astype(jnp.float32)
        return value

    def group_copy(level, phase, src, dst, size, d):
        rank = lax.rem(c, size)
        to = c - rank + lax.rem(rank + d, size)
        return pltpu.make_async_remote_copy(
            src_ref=src,
            dst_ref=dst,
            send_sem=cube_send.at[level, phase, d],
            recv_sem=cube_recv.at[level, phase, d],
            device_id={"cube": to},
            device_id_type=MESH,
        )

    def share_front(level, size, source):
        rank = lax.rem(c, size)
        if source is not None:
            front[level][rank] = source
        if size > 1:
            copy = lambda d: group_copy(
                level, 0, front[level].at[rank], front[level].at[rank], size, d
            )
            each(1, size, lambda d: copy(d).start())
            each(1, size, lambda d: copy(d).wait_recv())
            pending.append((1, size, copy))

    def interleave(chunk):
        step = min(128, chunk.shape[1])
        lane_in = lax.broadcasted_iota(jnp.int32, (step, 4 * step), 0)
        lane_out = lax.broadcasted_iota(jnp.int32, (step, 4 * step), 1)
        turned = jnp.where(lane_out < 2 * step, lane_out, lane_out - 2 * step - 1)
        expand = (turned == 2 * lane_in).astype(jnp.float32).astype(jnp.bfloat16)
        halves = []
        for at in range(0, chunk.shape[1], step):
            both = mm(chunk[:, at : at + step], expand, NN).astype(jnp.bfloat16)
            halves.append(jnp.concatenate([both[:, : 2 * step], both[:, 2 * step :]], axis=0))
        return jnp.concatenate(halves, axis=1)

    share_front(3, first_size, None)

    for at, level in enumerate(LEVELS):
        size, rows, part = geometry[level]
        wide = size * width
        rank = lax.rem(c, size)
        stripe = front[level].shape[3]
        top = front[level][:, 0].reshape(wide, stripe)
        if not level:
            pick = compact()
            top = mm(pick.astype(jnp.bfloat16), top, NN).astype(jnp.bfloat16)
            wide = top.shape[0]
        loads[level][0].wait()

        def term(z, core, level=level, part=part, top=top):
            at_row = pl.multiple_of((2 * z + core) * part, part)
            return mm(top, inv[level][pl.ds(at_row, part), :], NT)

        def panel_copy(kind, src, dst, d, z, core, level=level):
            return pltpu.make_async_remote_copy(
                src_ref=src,
                dst_ref=dst,
                send_sem=panel_send.at[level, kind, d],
                recv_sem=panel_recv.at[level, kind, d],
                device_id={"panel": 2 * z + core},
                device_id_type=MESH,
            )

        def to_twin(d, level=level, panel_copy=panel_copy):
            return panel_copy(0, twin_sent[level].at[d], twin_got[level].at[d], d, chip, 1 - core)

        def scatter(d, level=level, panel_copy=panel_copy):
            to = lax.rem(chip + d, chips)
            return panel_copy(1, sent[level].at[d], got[level].at[d], d, to, 1 - core)

        def send_twin(d, side, level=level, term=term, to_twin=to_twin):
            twin_sent[level][d] = term(lax.rem(chip + d, chips), side).astype(jnp.bfloat16)
            to_twin(d).start()

        def send_term(d, level=level, term=term, to_twin=to_twin, scatter=scatter):
            mine = term(lax.rem(chip + d, chips), 1 - core)
            to_twin(d).wait_recv()
            sent[level][d] = (mine + twin_got[level][d].astype(jnp.float32)).astype(jnp.bfloat16)
            scatter(d).start()

        each(1, chips, lambda d, send_twin=send_twin: send_twin(d, core))
        send_twin(0, 1 - core)
        each(1, chips, send_term)
        own = term(chip, core)
        to_twin(0).wait_recv()
        own = own + twin_got[level][0].astype(jnp.float32)
        for d in range(1, chips):
            scatter(d).wait_recv()
            own = own + got[level][d].astype(jnp.float32)
        own = own.astype(jnp.bfloat16)
        full[level][chip, core] = own

        def gather(d, level=level, panel_copy=panel_copy):
            here = full[level].at[chip, core]
            return panel_copy(2, here, here, d, lax.rem(chip + d, chips), 1 - core)

        def forward(d, side, level=level, panel_copy=panel_copy):
            here = full[level].at[lax.rem(chip + chips - d, chips), side]
            return panel_copy(3, here, here, d, chip, 1 - core)

        each(1, chips, lambda d, gather=gather: gather(d).start())
        forward(0, core).start()
        proj_out[level][...] = own
        if not level:
            pick_out[...] = pick
        if level == 3 and size == 1:
            each(1, cube, lambda d: route(d, 1).wait_recv())
            for j in range(1, 4):
                settle_block(j)
        pending.append((0, chips, to_twin))
        pending.append((1, chips, scatter))
        pending.append((1, chips, gather))
        pending.append((0, 1, lambda d, forward=forward: forward(d, core)))
        pending.append((1, chips, lambda d, forward=forward: forward(d, 1 - core)))

        if level:
            loads[level][1].wait()

        def add_chunk(z, core, first, level=level, part=part, wide=wide, stripe=stripe):
            chunk = full[level][z, core]
            value = mm(chunk, chunk, NT)
            gram[level][...] = value if first else gram[level][...] + value
            at_row = pl.multiple_of((2 * z + core) * part, part)
            if level == 2:
                value = mm(interleave(chunk), coup[2][pl.ds(at_row, part)].reshape(2 * part, stripe), NN)
                value = value.reshape(2, wide, stripe)
                cross[2][...] = value if first else cross[2][...] + value
                return
            for j in range(level):
                value = mm(chunk, coup[level][j, pl.ds(at_row, part), :], NN)
                cross[level][j] = value if first else cross[level][j] + value

        add_chunk(chip, core, True)

        def receive(d, gather=gather, forward=forward, add_chunk=add_chunk):
            gather(d).wait_recv()
            forward(d, 1 - core).start()
            add_chunk(lax.rem(chip + chips - d, chips), 1 - core, False)

        def receive_twin(d, side, forward=forward, add_chunk=add_chunk):
            forward(d, 1 - side).wait_recv()
            add_chunk(lax.rem(chip + chips - d, chips), side, False)

        receive_twin(0, 1 - core)
        each(1, chips, receive)
        each(1, chips, lambda d, receive_twin=receive_twin: receive_twin(d, core))

        steps = radices(size)
        stride = 1
        copies = None
        for stage, radix in enumerate(steps):
            if stage and level:
                settle(copies[1], radix_before)
                cross[level][...] = fold(cross_part[level], stage - 1, radix_before)
            digit = lax.rem(lax.div(rank, stride), radix)
            copies = []
            for kind, slots, acc in ((0, gram_part, gram), (1, cross_part, cross)):
                if kind and not level:
                    continue
                slots[level][stage, digit] = acc[level][...].astype(slots[level].dtype)

                def copy(d, kind=kind, slot=slots[level], stage=stage, digit=digit, stride=stride, radix=radix, level=level):
                    return pltpu.make_async_remote_copy(
                        src_ref=slot.at[stage, digit],
                        dst_ref=slot.at[stage, digit],
                        send_sem=cube_send.at[level, 1 + 2 * stage + kind, d],
                        recv_sem=cube_recv.at[level, 1 + 2 * stage + kind, d],
                        device_id=(
                            c + (lax.rem(digit + d, radix) - digit) * stride,
                            p if kind else p + 1 - 2 * core,
                        ),
                        device_id_type=MESH,
                    )

                each(1, radix, lambda d, copy=copy: copy(d).start())
                pending.append((1, radix, copy))
                copies.append(copy)
            settle(copies[0], radix)
            gram[level][...] = fold(gram_part[level], stage, radix)
            radix_before, stride = radix, stride * radix
        total = eye(wide) + gram[level][...]
        if not level:
            gram_out[...] = total
            break
        blocks = factor_panels(total, width, work)
        if steps:
            settle(copies[1], radix_before)
            summed_all = fold(cross_part[level], len(steps) - 1, radix_before)
        for j in range(level):
            summed = summed_all[j] if steps else cross[level][j]
            for k, (_, inverse, below) in enumerate(blocks):
                low = k * width
                right = front[level][k, j + 1].astype(jnp.float32) - summed[low : low + width]
                for earlier_k in range(k):
                    at_row = (k - earlier_k - 1) * width
                    right = right - mm32(
                        blocks[earlier_k][2][at_row : at_row + width], values[earlier_k], NN
                    )
                values = [] if k == 0 else values
                values.append(mm32(inverse, right, NN))
                solved[level][k, j] = values[k].astype(jnp.bfloat16)
        share_front(level - 1, geometry[level - 1][0], solved[level][rank])

    for rest in (0, 1):
        each(1, cube, lambda d, rest=rest: route(d, rest).wait_send())
    each(1, cube, lambda d: tell(d).wait_send())
    for low, high, copy in pending:
        each(low, high, lambda d, copy=copy: copy(d).wait_send())


def finish(width, total, pick, root, leaf, middle, upper, core_out, root_out, *refs):
    results, (work, low_factor, sems) = refs[:3], refs[3:]
    copies = [
        pltpu.make_async_copy(source, result, sems.at[k])
        for k, (source, result) in enumerate(zip((leaf, middle, upper), results))
    ]
    for copy in copies:
        copy.start()
    chosen = pick[...]
    wide, slots = chosen.shape
    low_factor[...] = jnp.zeros(low_factor.shape, jnp.float32)
    for k, (upper_part, _, below) in enumerate(factor_panels(total[...], width, work)):
        low = k * width
        low_factor[low : low + width, low : low + width] = mm32(eye(width), upper_part, NT)
        if below is not None:
            low_factor[low + width :, low : low + width] = below
    spread = mm32(low_factor[...], chosen, NN)
    narrow = chosen.astype(jnp.bfloat16)
    used = mm(narrow, jnp.ones((wide, slots), jnp.bfloat16), TN)
    core_out[...] = mm32(chosen, spread, TN) + eye(slots) * (1.0 - used)
    root_out[...] = mm(narrow, root[...], TN).astype(jnp.bfloat16)
    for copy in copies:
        copy.wait()


def body(
    cube,
    panel,
    columns,
    leaf_of,
    inverse_root,
    inverse_upper,
    inverse_middle,
    inverse_leaf,
    coupling_upper,
    coupling_middle,
    coupling_leaf,
):
    time_cols, _, stripe = columns.shape
    leaves = min(8, cube)
    leaf_share = cube // leaves
    per_slot = max(1, (2 * time_cols // leaves + leaf_share - 1) // leaf_share)
    width = cube * per_slot
    inverses = [inverse_leaf, inverse_middle, inverse_upper, inverse_root]
    couplings = [
        jnp.transpose(coupling_leaf, (1, 0, 2)),
        coupling_middle,
        jnp.transpose(coupling_upper, (1, 0, 2)),
    ]
    geometry = {}
    for level, inverse in zip(LEVELS, inverses):
        rows = inverse.shape[0]
        geometry[level] = (cube // min(2**level, cube), rows, rows // panel)
    wide = {level: geometry[level][0] * width for level in LEVELS}
    ranks = cube * time_cols
    slots = wide[0]
    wide[0] = ranks
    part = {level: geometry[level][2] for level in LEVELS}
    size = {level: geometry[level][0] for level in LEVELS}
    vm = pltpu.VMEM
    scratch = [vm(x.shape, x.dtype) for x in inverses]
    scratch += [vm(x.shape, x.dtype) for x in couplings]
    scratch += [vm((cube, 4, SLOT, stripe), jnp.bfloat16)] * 2
    scratch += [vm((8, 128), jnp.int32), vm((cube, 8, 128), jnp.int32)]
    scratch += [vm((size[l], l + 1, width, stripe), jnp.bfloat16) for l in LEVELS]
    for _ in range(4):
        scratch += [vm((panel // 2, wide[l], part[l]), jnp.bfloat16) for l in LEVELS]
    scratch += [vm((panel // 2, 2, wide[l], part[l]), jnp.bfloat16) for l in LEVELS]
    scratch += [vm((wide[l], wide[l]), jnp.float32) for l in LEVELS]
    for l in LEVELS:
        steps = radices(size[l]) or [1]
        kind = jnp.float32 if size[l] <= 2 else jnp.bfloat16
        scratch += [vm((len(steps), max(steps), wide[l], wide[l]) if size[l] > 1 else (1, 1, 8, 128), kind)]
    scratch += [vm((l, wide[l], stripe), jnp.float32) for l in LEVELS[:3]]
    for l in LEVELS[:3]:
        steps = radices(size[l]) or [1]
        scratch += [vm((len(steps), max(steps), l, wide[l], stripe), jnp.bfloat16)]
    scratch += [vm((size[l], l, width, stripe), jnp.bfloat16) for l in LEVELS[:3]]
    scratch += [vm((width, 128), jnp.float32)]
    dma = pltpu.SemaphoreType.DMA
    scratch += [dma((4, 2)), dma((2, cube)), dma((2, cube)), dma((cube,)), dma((cube,)), dma((4, 4, panel // 2)), dma((4, 4, panel // 2))]
    scratch += [dma((4, 5, cube)), dma((4, 5, cube))]
    shape = jax.ShapeDtypeStruct
    passed = [shape((wide[l], part[l]), jnp.bfloat16) for l in LEVELS]
    outs = [shape((ranks, ranks), jnp.float32), shape((ranks, slots), jnp.float32)] + passed
    in_vmem = pl.BlockSpec(memory_space=pltpu.VMEM)
    in_any = pl.BlockSpec(memory_space=pl.ANY)
    total, pick, leaf, middle, upper, root = pl.pallas_call(
        functools.partial(kernel, cube, panel, width, per_slot, leaves, geometry),
        out_shape=outs,
        in_specs=[in_vmem, in_vmem] + [in_any] * 7,
        out_specs=[in_vmem] * 6,
        scratch_shapes=scratch,
        compiler_params=pltpu.CompilerParams(
            collective_id=0, has_side_effects=True, vmem_limit_bytes=58 * 2**20
        ),
    )(
        jnp.transpose(leaf_of),
        columns,
        *inverses,
        *couplings,
    )
    core, root, leaf, middle, upper = pl.pallas_call(
        functools.partial(finish, width),
        out_shape=[shape((slots, slots), jnp.float32), shape((slots, part[0]), jnp.bfloat16)]
        + passed[:3],
        in_specs=[in_vmem] * 3 + [in_any] * 3,
        out_specs=[in_vmem] * 2 + [in_any] * 3,
        scratch_shapes=[vm((width, 128), jnp.float32), vm((ranks, ranks), jnp.float32), dma((3,))],
    )(total, pick, root, leaf, middle, upper)
    return (core, root.T, upper.T, middle.T, leaf.T)


def solution(mesh):
    in_specs = (
        P("cube", None, "panel"),
        P("cube", None),
        P("cube", "panel"),
        P("cube", "panel"),
        P("cube", "panel"),
        P("cube", "panel"),
        P("cube", None, "panel"),
        P("cube", None, "panel"),
        P("cube", None, "panel"),
    )
    out_specs = (
        P(),
        P(("cube", "panel"), None),
        P(("cube", "panel"), None),
        P(("cube", "panel"), None),
        P(("cube", "panel"), None),
    )
    run = functools.partial(body, mesh.shape["cube"], mesh.shape["panel"])
    return jax.shard_map(run, mesh=mesh, in_specs=in_specs, out_specs=out_specs, check_vma=False)
```

```python
import functools

import jax
import jax.numpy as jnp
from jax import lax
from jax.experimental import pallas as pl
from jax.experimental.pallas import tpu as pltpu
from jax.sharding import PartitionSpec as P

MESH = pl.DeviceIdType.MESH
LEVELS = (3, 2, 1, 0)
SLOT = 16
NT = (((1,), (1,)), ((), ()))
NN = (((1,), (0,)), ((), ()))
TN = (((0,), (0,)), ((), ()))


def radices(size):
    steps = []
    while size > 1:
        steps.append(min(4, size))
        size //= steps[-1]
    return steps


def mm(a, b, dims):
    return lax.dot_general(a, b, dims, preferred_element_type=jnp.float32)


def mm32(a, b, dims):
    return lax.dot_general(
        a, b, dims, precision=lax.Precision.HIGHEST, preferred_element_type=jnp.float32
    )


def factor_block(block, work):
    n = block.shape[0]
    work[:, :n] = block
    row_pos = lax.broadcasted_iota(jnp.int32, (n, 128), 0)
    lane_pos = lax.broadcasted_iota(jnp.int32, (n, 128), 1)
    m = jnp.where(lane_pos < n, work[...], 0.0) + (lane_pos == row_pos + 64).astype(jnp.float32)
    done = []
    for base in range(0, n, 8):
        if base:
            done.append(m[:8])
            m = m[8:]
        shape = m.shape
        here = row_pos[: shape[0]]
        columns = [jnp.broadcast_to(m[:, base + at : base + at + 1], shape) for at in range(8)]
        for at in range(0, 8, 2):
            first, second = columns[at], columns[at + 1]
            a, b, d = first[at : at + 1], first[at + 1 : at + 2], second[at + 1 : at + 2]
            over_a, over_d = 1.0 / a, a * (1.0 / (a * d - b * b))
            ratio = b * over_a
            low = jnp.where(here > at + 1, (second - ratio * first) * over_d, 0.0)
            first = jnp.where(here > at, first * over_a, 0.0)

            def reduced(value):
                top, next_row = value[at : at + 1], value[at + 1 : at + 2]
                return value - first * top - low * (next_row - ratio * top)

            for k in range(at + 2, 8):
                columns[k] = reduced(columns[k])
            m = reduced(m)
    m = jnp.concatenate(done + [m], axis=0)
    pivots = jnp.sum(jnp.where(lane_pos == row_pos, m, 0.0), axis=1, keepdims=True)
    m = m * lax.rsqrt(pivots)
    upper = jnp.where(lane_pos >= row_pos, m, 0.0)[:, :n]
    return upper, m[:, 64 : 64 + n]


def eye(n):
    return (
        lax.broadcasted_iota(jnp.int32, (n, n), 0) == lax.broadcasted_iota(jnp.int32, (n, n), 1)
    ).astype(jnp.float32)


def factor_panels(total, width, work):
    count = total.shape[0] // width
    panels = [total[k * width :, k * width : (k + 1) * width] for k in range(count)]
    result = []
    for k in range(count):
        upper, inverse = factor_block(panels[k][:width], work)
        below = None
        if k + 1 < count:
            below = mm32(panels[k][width:], inverse, NT)
            for j in range(k + 1, count):
                at = (j - k - 1) * width
                panels[j] = panels[j] - mm32(below[at:], below[at : at + width], NT)
        result.append((upper, inverse, below))
    return result


def kernel(cube, panel, width, per_slot, leaves, geometry, *refs):
    refs = list(refs)
    take = lambda count: [refs.pop(0) for _ in range(count)]
    labels, columns = take(2)
    inv_hbm = dict(zip(LEVELS, take(4)))
    coup_hbm = dict(zip(LEVELS[:3], take(3)))
    gram_out, pick_out = take(2)
    proj_out = dict(zip(LEVELS, take(4)))
    inv = dict(zip(LEVELS, take(4)))
    coup = dict(zip(LEVELS[:3], take(3)))
    packed, arrived, place, places = take(4)
    tops = dict(zip(LEVELS[:3], take(3)))
    parts = take(1)[0]
    rest = dict(zip(LEVELS[:3], take(3)))
    linv = dict(zip(LEVELS[1:], take(3)))
    all_linv = dict(zip(LEVELS[:3], take(3)))
    all_tops = dict(zip(LEVELS[:3], take(3)))
    twin_sent = dict(zip(LEVELS, take(4)))
    twin_got = dict(zip(LEVELS, take(4)))
    sent = dict(zip(LEVELS, take(4)))
    got = dict(zip(LEVELS, take(4)))
    full = dict(zip(LEVELS, take(4)))
    gram = dict(zip(LEVELS, take(4)))
    gram_part = dict(zip(LEVELS, take(4)))
    cross = dict(zip(LEVELS[:3], take(3)))
    cross_part = dict(zip(LEVELS[:3], take(3)))
    work = take(1)[0]
    load_sem, route_send, route_recv, place_send, place_recv, panel_send, panel_recv, cube_send, cube_recv = take(9)

    c = lax.axis_index("cube")
    p = lax.axis_index("panel")
    chips = panel // 2
    chip, core = lax.div(p, 2), lax.rem(p, 2)

    loads = {}
    for at, level in enumerate(LEVELS):
        loads[level, 0] = pltpu.make_async_copy(inv_hbm[level], inv[level], load_sem.at[at, 0])
    for at, level in ((1, 2), (2, 1)):
        loads[level, 1] = pltpu.make_async_copy(coup_hbm[level], coup[level], load_sem.at[at, 1])
    for j in range(3):
        loads[3, 1 + j] = pltpu.make_async_copy(
            coup_hbm[3].at[j], coup[3].at[j], load_sem.at[0, 1 + j]
        )
    loads[3, 0].start()

    barrier = pltpu.get_barrier_semaphore()

    def greet(axis, me, size):
        def one(d, carry):
            pl.semaphore_signal(
                barrier, inc=1, device_id={axis: lax.rem(me + d, size)}, device_id_type=MESH
            )
            return carry

        lax.fori_loop(1, size, one, 0)

    greet("cube", c, cube)
    greet("panel", p, panel)

    def greet_across(d, carry):
        pl.semaphore_signal(
            barrier, inc=1, device_id=(lax.rem(c + d, cube), p + 1 - 2 * core), device_id_type=MESH
        )
        return carry

    lax.fori_loop(1, cube, greet_across, 0)

    label = labels[...]
    time_cols = label.shape[1]
    share = cube // leaves
    onehot = lax.broadcasted_iota(jnp.int32, (16, time_cols), 0) == label
    earlier = lax.broadcasted_iota(jnp.int32, (time_cols, time_cols), 0) < (
        lax.broadcasted_iota(jnp.int32, (time_cols, time_cols), 1)
    )
    onehot = onehot.astype(jnp.float32)
    before = mm(onehot.astype(jnp.bfloat16), earlier.astype(jnp.float32).astype(jnp.bfloat16), NN)
    within = jnp.sum(before * onehot, axis=0, keepdims=True).astype(jnp.int32)
    turn = jnp.zeros_like(within)
    for step in range(1, share):
        turn = turn + (within >= step * per_slot).astype(jnp.int32)
    target = (label * share + turn) * (4 * SLOT) + within - turn * per_slot
    slot = (label * share + turn) * width + c * per_slot + within - turn * per_slot
    place[...] = jnp.zeros(place.shape, jnp.int32)
    place[:1, :time_cols] = slot
    stretch = (
        lax.broadcasted_iota(jnp.int32, (time_cols, 4 * time_cols), 0)
        == lax.div(lax.broadcasted_iota(jnp.int32, (time_cols, 4 * time_cols), 1), 4)
    ).astype(jnp.float32)
    sent_to = jnp.broadcast_to(target.astype(jnp.float32), (8, time_cols))
    sent_to = mm32(sent_to, stretch, NN)[:1] + 0.5
    kind_at = lax.rem(lax.broadcasted_iota(jnp.int32, (1, 4 * time_cols), 1), 4)
    sent_to = sent_to.astype(jnp.int32) + kind_at * SLOT
    dispatch = (
        (lax.broadcasted_iota(jnp.int32, (cube * 4 * SLOT, 4 * time_cols), 0) == sent_to)
        .astype(jnp.float32)
        .astype(jnp.bfloat16)
    )
    stripe = columns.shape[2]
    by_time = columns[...].reshape(4 * time_cols, stripe)
    packed[...] = mm(dispatch, by_time, NN).astype(jnp.bfloat16).reshape(cube, 4, SLOT, stripe)

    pl.semaphore_wait(barrier, 2 * cube + panel - 3)
    for load in ((3, 1), (2, 0), (3, 2), (3, 3), (2, 1), (1, 0), (1, 1), (0, 0)):
        loads[load].start()

    def route(d, rest):
        to = lax.rem(c + d, cube)
        blocks = pl.ds(1, 3) if rest else pl.ds(0, 1)
        return pltpu.make_async_remote_copy(
            src_ref=packed.at[to, blocks],
            dst_ref=arrived.at[c, blocks],
            send_sem=route_send.at[rest, d],
            recv_sem=route_recv.at[rest, d],
            device_id={"cube": to},
            device_id_type=MESH,
        )

    def each(low, high, do):
        def one(d, carry):
            do(d)
            return carry

        lax.fori_loop(low, high, one, 0)

    def tell(d):
        return pltpu.make_async_remote_copy(
            src_ref=place,
            dst_ref=places.at[c],
            send_sem=place_send.at[d],
            recv_sem=place_recv.at[d],
            device_id={"cube": lax.rem(c + d, cube)},
            device_id_type=MESH,
        )

    each(1, cube, lambda d: route(d, 0).start())
    each(1, cube, lambda d: route(d, 1).start())
    each(1, cube, lambda d: tell(d).start())
    arrived[c] = packed[c]
    places[c] = place[...]
    each(1, cube, lambda d: route(d, 0).wait_recv())
    out_pos = lax.broadcasted_iota(jnp.int32, (width, cube * SLOT), 0)
    in_pos = lax.broadcasted_iota(jnp.int32, (width, cube * SLOT), 1)
    select = jnp.zeros((width, cube * SLOT), jnp.float32)
    for s in range(cube):
        hit = (in_pos - s * SLOT == out_pos - s * per_slot) & (out_pos >= s * per_slot)
        hit = hit & (out_pos < (s + 1) * per_slot)
        select = select + hit.astype(jnp.float32)
    select = select.astype(jnp.bfloat16)
    first_size = geometry[3][0]
    pending = []

    def settle_block(j):
        mine = mm(select, arrived[:, j].reshape(cube * SLOT, stripe), NN)
        return mine.astype(jnp.bfloat16)

    def compact():
        each(1, cube, lambda d: tell(d).wait_recv())
        wide = cube * width
        slot_pos = lax.broadcasted_iota(jnp.int32, (wide, time_cols), 0)
        ones = jnp.ones((8, time_cols), jnp.bfloat16)
        used = jnp.zeros((8, wide), jnp.float32)
        for s in range(cube):
            at_slot = (slot_pos == places[s, :1, :time_cols]).astype(jnp.float32)
            used = used + mm(ones, at_slot.astype(jnp.bfloat16), NT)
        ahead = lax.broadcasted_iota(jnp.int32, (wide, wide), 0) < (
            lax.broadcasted_iota(jnp.int32, (wide, wide), 1)
        )
        count = mm(used.astype(jnp.bfloat16), ahead.astype(jnp.float32).astype(jnp.bfloat16), NN)
        row = lax.broadcasted_iota(jnp.int32, (cube * time_cols, wide), 0)
        hit = (row == count[:1].astype(jnp.int32)) & (used[:1] > 0.5)
        return hit.astype(jnp.float32)

    def interleave(chunk):
        step = min(128, chunk.shape[1])
        lane_in = lax.broadcasted_iota(jnp.int32, (step, 4 * step), 0)
        lane_out = lax.broadcasted_iota(jnp.int32, (step, 4 * step), 1)
        turned = jnp.where(lane_out < 2 * step, lane_out, lane_out - 2 * step - 1)
        expand = (turned == 2 * lane_in).astype(jnp.float32).astype(jnp.bfloat16)
        halves = []
        for at in range(0, chunk.shape[1], step):
            both = mm(chunk[:, at : at + step], expand, NN).astype(jnp.bfloat16)
            halves.append(jnp.concatenate([both[:, : 2 * step], both[:, 2 * step :]], axis=0))
        return jnp.concatenate(halves, axis=1)

    def fold(slots, stage, radix):
        value = slots[stage, 0].astype(jnp.float32)
        for s in range(1, radix):
            value = value + slots[stage, s].astype(jnp.float32)
        return value

    def group_copy(level, phase, block, d):
        size = geometry[level][0]
        rank = lax.rem(c, size)
        return pltpu.make_async_remote_copy(
            src_ref=block,
            dst_ref=block,
            send_sem=cube_send.at[level, phase, d],
            recv_sem=cube_recv.at[level, phase, d],
            device_id={"cube": c - rank + lax.rem(rank + d, size)},
            device_id_type=MESH,
        )

    shared = {}

    def share(level, phase, block):
        size = geometry[level][0]
        copy = lambda d: group_copy(level, phase, block, d)
        each(1, size, lambda d: copy(d).start())
        pending.append((1, size, copy))
        shared[level, phase] = copy

    def shared_wait(level, phase):
        copy = shared[level, phase]
        each(1, geometry[level][0], lambda d: copy(d).wait_recv())

    def all_sum(level, kind, slots, acc):
        size = geometry[level][0]
        rank = lax.rem(c, size)
        stride = 1
        for stage, radix in enumerate(radices(size)):
            digit = lax.rem(lax.div(rank, stride), radix)
            slots[stage, digit] = acc[...].astype(slots.dtype)

            def copy(d, stage=stage, digit=digit, stride=stride, radix=radix):
                return pltpu.make_async_remote_copy(
                    src_ref=slots.at[stage, digit],
                    dst_ref=slots.at[stage, digit],
                    send_sem=cube_send.at[level, 1 + 2 * stage + kind, d],
                    recv_sem=cube_recv.at[level, 1 + 2 * stage + kind, d],
                    device_id=(
                        c + (lax.rem(digit + d, radix) - digit) * stride,
                        p if kind else p + 1 - 2 * core,
                    ),
                    device_id_type=MESH,
                )

            each(1, radix, lambda d, copy=copy: copy(d).start())
            pending.append((1, radix, copy))
            each(1, radix, lambda d, copy=copy: copy(d).wait_recv())
            acc[...] = fold(slots, stage, radix)
            stride = stride * radix

    def own_rows(level, rows, store):
        if geometry[level][0] == 1:
            return rows
        store[...] = rows.reshape(store.shape).astype(store.dtype)
        return store[lax.rem(c, geometry[level][0])]

    def chunks(level):
        return [full[level][z, k] for z in range(panel // 2) for k in range(2)]

    def other_cross(level):
        part = geometry[level][2]
        if level == 3:
            for j in range(1, 3):
                loads[3, 1 + j].wait()
                value = None
                for at, chunk in enumerate(chunks(3)):
                    term = mm(chunk, coup[3][j, at * part : (at + 1) * part, :], NN)
                    value = term if value is None else value + term
                cross[3][j] = value

    def close(level):
        size = geometry[level][0]
        wide = size * width
        value = None
        for chunk in chunks(level):
            term = mm(chunk, chunk, NT)
            value = term if value is None else value + term
        gram[level][...] = value
        all_sum(level, 0, gram_part[level], gram[level])
        blocks = factor_panels(eye(wide) + gram[level][...], width, work)
        rows = []
        for k, (_, inverse, _) in enumerate(blocks):
            right = None
            for e in range(k):
                at_row = (k - e - 1) * width
                term = mm32(blocks[e][2][at_row : at_row + width], rows[e], NN)
                right = term if right is None else right + term
            here = (
                lax.broadcasted_iota(jnp.int32, (width, wide), 1)
                == lax.broadcasted_iota(jnp.int32, (width, wide), 0) + k * width
            ).astype(jnp.float32)
            rows.append(mm32(inverse, here if right is None else here - right, NN))
        mine = own_rows(level, jnp.concatenate(rows, axis=0), all_linv[level])
        after = geometry[level - 1][0]
        at = lax.rem(c, after)
        linv[level - 1][at] = mine
        share(level - 1, 5, linv[level - 1].at[at])
        if size == 1:
            other_cross(level)
        for j in range(1, level):
            right = rest[level][:, j].reshape(wide, stripe).astype(jnp.float32) - cross[level][j]
            rest[level - 1][at, j - 1] = mm32(mine, right, NN).astype(jnp.bfloat16)
        if level > 1:
            share(level - 1, 6, rest[level - 1].at[at])

    def open_rest():
        each(1, cube, lambda d: route(d, 1).wait_recv())
        at = lax.rem(c, first_size)
        for j in range(3):
            rest[3][at, j] = settle_block(j + 1)
        share(3, 6, rest[3].at[at])

    tops[3][lax.rem(c, first_size)] = settle_block(0)
    share(3, 0, tops[3].at[lax.rem(c, first_size)])
    later = open_rest

    for at, level in enumerate(LEVELS):
        size, rows, part = geometry[level]
        if size > 1:
            later()
            later = None
        shared_wait(level, 0)
        if level:
            wide = size * width
            top = tops[level][...].reshape(wide, stripe)
        else:
            pick = compact()
            below = geometry[1][0] * width
            sides = [
                pick[:, g * below : (g + 1) * below] for g in range(cube // geometry[1][0])
            ]
            top = None
            for s in range(cube):
                value = mm(sides[s // geometry[1][0]].astype(jnp.bfloat16), parts[s], NN)
                top = value if top is None else top + value
            top = top.astype(jnp.bfloat16)
            wide = top.shape[0]
        loads[level, 0].wait()

        def term(z, core, level=level, part=part, top=top):
            at_row = pl.multiple_of((2 * z + core) * part, part)
            return mm(top, inv[level][pl.ds(at_row, part), :], NT)

        def panel_copy(kind, src, dst, d, z, core, level=level):
            return pltpu.make_async_remote_copy(
                src_ref=src,
                dst_ref=dst,
                send_sem=panel_send.at[level, kind, d],
                recv_sem=panel_recv.at[level, kind, d],
                device_id={"panel": 2 * z + core},
                device_id_type=MESH,
            )

        def to_twin(d, level=level, panel_copy=panel_copy):
            return panel_copy(0, twin_sent[level].at[d], twin_got[level].at[d], d, chip, 1 - core)

        def scatter(d, level=level, panel_copy=panel_copy):
            to = lax.rem(chip + d, chips)
            return panel_copy(1, sent[level].at[d], got[level].at[d], d, to, 1 - core)

        def send_twin(d, side, level=level, term=term, to_twin=to_twin):
            twin_sent[level][d] = term(lax.rem(chip + d, chips), side).astype(jnp.bfloat16)
            to_twin(d).start()

        def send_term(d, level=level, term=term, to_twin=to_twin, scatter=scatter):
            mine = term(lax.rem(chip + d, chips), 1 - core)
            to_twin(d).wait_recv()
            sent[level][d] = (mine + twin_got[level][d].astype(jnp.float32)).astype(jnp.bfloat16)
            scatter(d).start()

        for d in range(1, chips):
            send_twin(d, core)
        send_twin(0, 1 - core)
        for d in range(1, chips):
            send_term(d)
        own = term(chip, core)
        if later is not None:
            later()
        to_twin(0).wait_recv()
        own = own + twin_got[level][0].astype(jnp.float32)
        if level < 3:
            shared_wait(level, 5)
            child = geometry[level + 1][0]
            inner = child * width
            nodes = size // child
            lower = [
                linv[level][n * child : (n + 1) * child].reshape(inner, inner)
                for n in range(nodes)
            ]
            if not level:
                scale = None
                for n in range(nodes):
                    value = mm32(sides[n], mm32(lower[n], sides[n], NT), NN)
                    scale = value if scale is None else scale + value
        for d in range(1, chips):
            scatter(d).wait_recv()
            own = own + got[level][d].astype(jnp.float32)
        if not level:
            own = mm32(scale, own, NN)
        elif level < 3:
            own = jnp.concatenate(
                [mm32(lower[n], own[n * inner : (n + 1) * inner], NN) for n in range(nodes)], axis=0
            )
        own = own.astype(jnp.bfloat16)
        full[level][chip, core] = own

        def gather(d, level=level, panel_copy=panel_copy):
            here = full[level].at[chip, core]
            return panel_copy(2, here, here, d, lax.rem(chip + d, chips), 1 - core)

        def forward(d, side, level=level, panel_copy=panel_copy):
            here = full[level].at[lax.rem(chip + chips - d, chips), side]
            return panel_copy(3, here, here, d, chip, 1 - core)

        each(1, chips, lambda d, gather=gather: gather(d).start())
        forward(0, core).start()
        proj_out[level][...] = own
        if not level:
            pick_out[...] = pick
        pending.append((0, chips, to_twin))
        pending.append((1, chips, scatter))
        pending.append((1, chips, gather))
        pending.append((0, 1, lambda d, forward=forward: forward(d, core)))
        pending.append((1, chips, lambda d, forward=forward: forward(d, 1 - core)))

        if level:
            loads[level, 1].wait()

        def add_chunk(z, core, first, level=level, part=part, wide=wide):
            chunk = full[level][z, core]
            at_row = pl.multiple_of((2 * z + core) * part, part)
            if not level:
                value = mm(chunk, chunk, NT)
                gram[0][...] = value if first else gram[0][...] + value
            elif level == 2:
                value = mm(interleave(chunk), coup[2][pl.ds(at_row, part)].reshape(2 * part, stripe), NN)
                value = value.reshape(2, wide, stripe)
                cross[2][...] = value if first else cross[2][...] + value
            else:
                value = mm(chunk, coup[level][0, pl.ds(at_row, part), :], NN)
                cross[level][0] = value if first else cross[level][0] + value

        add_chunk(chip, core, True)

        def receive(d, gather=gather, forward=forward, add_chunk=add_chunk):
            gather(d).wait_recv()
            forward(d, 1 - core).start()
            add_chunk(lax.rem(chip + chips - d, chips), 1 - core, False)

        def receive_twin(d, side, forward=forward, add_chunk=add_chunk):
            forward(d, 1 - side).wait_recv()
            add_chunk(lax.rem(chip + chips - d, chips), side, False)

        receive_twin(0, 1 - core)
        for d in range(1, chips):
            receive(d)
        for d in range(1, chips):
            receive_twin(d, core)

        if not level:
            all_sum(0, 0, gram_part[0], gram[0])
            gram_out[...] = eye(wide) + gram[0][...]
            break
        shared_wait(level, 6)
        if level > 1 and size > 1:
            other_cross(level)
            all_sum(level, 1, cross_part[level], cross[level])
        right = rest[level][:, 0].reshape(wide, stripe).astype(jnp.float32)
        after = geometry[level - 1][0]
        at = lax.rem(c, after)
        if level > 1:
            right = (right - cross[level][0]).astype(jnp.bfloat16)
            tops[level - 1][at] = own_rows(level, right, all_tops[level])
            share(level - 1, 0, tops[level - 1].at[at])
        else:
            right = jnp.where(lax.rem(c, size) == 0, right, 0.0) - cross[1][0]
            parts[at] = right.astype(jnp.bfloat16)
            share(0, 0, parts.at[at])
        later = functools.partial(close, level)

    for block in (0, 1):
        each(1, cube, lambda d, block=block: route(d, block).wait_send())
    each(1, cube, lambda d: tell(d).wait_send())
    for low, high, copy in pending:
        each(low, high, lambda d, copy=copy: copy(d).wait_send())


def finish(width, total, pick, root, leaf, middle, upper, core_out, root_out, *refs):
    results, (work, low_factor, sems) = refs[:3], refs[3:]
    copies = [
        pltpu.make_async_copy(source, result, sems.at[k])
        for k, (source, result) in enumerate(zip((leaf, middle, upper), results))
    ]
    for copy in copies:
        copy.start()
    chosen = pick[...]
    wide, slots = chosen.shape
    low_factor[...] = jnp.zeros(low_factor.shape, jnp.float32)
    for k, (upper_part, _, below) in enumerate(factor_panels(total[...], width, work)):
        low = k * width
        low_factor[low : low + width, low : low + width] = mm32(eye(width), upper_part, NT)
        if below is not None:
            low_factor[low + width :, low : low + width] = below
    spread = mm32(low_factor[...], chosen, NN)
    narrow = chosen.astype(jnp.bfloat16)
    used = mm(narrow, jnp.ones((wide, slots), jnp.bfloat16), TN)
    core_out[...] = mm32(chosen, spread, TN) + eye(slots) * (1.0 - used)
    root_out[...] = mm(narrow, root[...], TN).astype(jnp.bfloat16)
    for copy in copies:
        copy.wait()


def body(
    cube,
    panel,
    columns,
    leaf_of,
    inverse_root,
    inverse_upper,
    inverse_middle,
    inverse_leaf,
    coupling_upper,
    coupling_middle,
    coupling_leaf,
):
    time_cols, _, stripe = columns.shape
    leaves = min(8, cube)
    leaf_share = cube // leaves
    per_slot = max(1, (2 * time_cols // leaves + leaf_share - 1) // leaf_share)
    width = cube * per_slot
    inverses = [inverse_leaf, inverse_middle, inverse_upper, inverse_root]
    couplings = [
        jnp.transpose(coupling_leaf, (1, 0, 2)),
        coupling_middle,
        jnp.transpose(coupling_upper, (1, 0, 2)),
    ]
    geometry = {}
    for level, inverse in zip(LEVELS, inverses):
        rows = inverse.shape[0]
        geometry[level] = (cube // min(2**level, cube), rows, rows // panel)
    wide = {level: geometry[level][0] * width for level in LEVELS}
    ranks = cube * time_cols
    slots = wide[0]
    wide[0] = ranks
    part = {level: geometry[level][2] for level in LEVELS}
    size = {level: geometry[level][0] for level in LEVELS}
    vm = pltpu.VMEM
    scratch = [vm(x.shape, x.dtype) for x in inverses]
    scratch += [vm(x.shape, x.dtype) for x in couplings]
    scratch += [vm((cube, 4, SLOT, stripe), jnp.bfloat16)] * 2
    scratch += [vm((8, 128), jnp.int32), vm((cube, 8, 128), jnp.int32)]
    scratch += [vm((size[l], width, stripe), jnp.bfloat16) for l in LEVELS[:3]]
    scratch += [vm((cube, wide[1], stripe), jnp.bfloat16)]
    scratch += [vm((size[l], l, width, stripe), jnp.bfloat16) for l in LEVELS[:3]]
    scratch += [vm((size[l], width, wide[l + 1]), jnp.float32) for l in LEVELS[1:]]
    scratch += [vm((size[l], width, wide[l]), jnp.float32) for l in LEVELS[:3]]
    scratch += [vm((size[l], width, stripe), jnp.bfloat16) for l in LEVELS[:3]]
    for _ in range(4):
        scratch += [vm((panel // 2, wide[l], part[l]), jnp.bfloat16) for l in LEVELS]
    scratch += [vm((panel // 2, 2, wide[l], part[l]), jnp.bfloat16) for l in LEVELS]
    scratch += [vm((wide[l], wide[l]), jnp.float32) for l in LEVELS]
    for l in LEVELS:
        steps = radices(size[l]) or [1]
        kind = jnp.float32 if size[l] <= 2 else jnp.bfloat16
        scratch += [vm((len(steps), max(steps), wide[l], wide[l]) if size[l] > 1 else (1, 1, 8, 128), kind)]
    scratch += [vm((l, wide[l], stripe), jnp.float32) for l in LEVELS[:3]]
    for l in LEVELS[:3]:
        steps = radices(size[l]) or [1]
        used = l > 1 and size[l] > 1
        scratch += [vm((len(steps), max(steps), l, wide[l], stripe) if used else (1, 1, 1, 16, 128), jnp.bfloat16)]
    scratch += [vm((width, 128), jnp.float32)]
    dma = pltpu.SemaphoreType.DMA
    scratch += [dma((4, 4)), dma((2, cube)), dma((2, cube)), dma((cube,)), dma((cube,)), dma((4, 4, panel // 2)), dma((4, 4, panel // 2))]
    scratch += [dma((4, 7, cube)), dma((4, 7, cube))]
    shape = jax.ShapeDtypeStruct
    passed = [shape((wide[l], part[l]), jnp.bfloat16) for l in LEVELS]
    outs = [shape((ranks, ranks), jnp.float32), shape((ranks, slots), jnp.float32)] + passed
    in_vmem = pl.BlockSpec(memory_space=pltpu.VMEM)
    in_any = pl.BlockSpec(memory_space=pl.ANY)
    total, pick, leaf, middle, upper, root = pl.pallas_call(
        functools.partial(kernel, cube, panel, width, per_slot, leaves, geometry),
        out_shape=outs,
        in_specs=[in_vmem, in_vmem] + [in_any] * 7,
        out_specs=[in_vmem] * 6,
        scratch_shapes=scratch,
        compiler_params=pltpu.CompilerParams(
            collective_id=0, has_side_effects=True, vmem_limit_bytes=58 * 2**20
        ),
    )(
        jnp.transpose(leaf_of),
        columns,
        *inverses,
        *couplings,
    )
    core, root, leaf, middle, upper = pl.pallas_call(
        functools.partial(finish, width),
        out_shape=[shape((slots, slots), jnp.float32), shape((slots, part[0]), jnp.bfloat16)]
        + passed[:3],
        in_specs=[in_vmem] * 6,
        out_specs=[in_vmem] * 2 + [in_any] * 3,
        scratch_shapes=[vm((width, 128), jnp.float32), vm((ranks, ranks), jnp.float32), dma((3,))],
    )(total, pick, root, leaf, middle, upper)
    return (core, root.T, upper.T, middle.T, leaf.T)


def solution(mesh):
    in_specs = (
        P("cube", None, "panel"),
        P("cube", None),
        P("cube", "panel"),
        P("cube", "panel"),
        P("cube", "panel"),
        P("cube", "panel"),
        P("cube", None, "panel"),
        P("cube", None, "panel"),
        P("cube", None, "panel"),
    )
    out_specs = (
        P(),
        P(("cube", "panel"), None),
        P(("cube", "panel"), None),
        P(("cube", "panel"), None),
        P(("cube", "panel"), None),
    )
    run = functools.partial(body, mesh.shape["cube"], mesh.shape["panel"])
    return jax.shard_map(run, mesh=mesh, in_specs=in_specs, out_specs=out_specs, check_vma=False)
```

```python
import functools

import jax
import jax.numpy as jnp
from jax import lax
from jax.experimental import pallas as pl
from jax.experimental.pallas import tpu as pltpu
from jax.sharding import PartitionSpec as P

MESH = pl.DeviceIdType.MESH
LEVELS = (3, 2, 1, 0)
SLOT = 16
NT = (((1,), (1,)), ((), ()))
NN = (((1,), (0,)), ((), ()))
TN = (((0,), (0,)), ((), ()))


def radices(size):
    steps = []
    while size > 1:
        steps.append(min(4, size))
        size //= steps[-1]
    return steps


def mm(a, b, dims):
    return lax.dot_general(a, b, dims, preferred_element_type=jnp.float32)


def mm32(a, b, dims):
    return lax.dot_general(
        a, b, dims, precision=lax.Precision.HIGHEST, preferred_element_type=jnp.float32
    )


def factor_block(block, work):
    n = block.shape[0]
    work[:, :n] = block
    row_pos = lax.broadcasted_iota(jnp.int32, (n, 128), 0)
    lane_pos = lax.broadcasted_iota(jnp.int32, (n, 128), 1)
    m = jnp.where(lane_pos < n, work[...], 0.0) + (lane_pos == row_pos + 64).astype(jnp.float32)
    done = []
    for base in range(0, n, 8):
        if base:
            done.append(m[:8])
            m = m[8:]
        shape = m.shape
        here = row_pos[: shape[0]]
        columns = [jnp.broadcast_to(m[:, base + at : base + at + 1], shape) for at in range(8)]
        for at in range(0, 8, 2):
            first, second = columns[at], columns[at + 1]
            a, b, d = first[at : at + 1], first[at + 1 : at + 2], second[at + 1 : at + 2]
            over_a, over_d = 1.0 / a, a * (1.0 / (a * d - b * b))
            ratio = b * over_a
            low = jnp.where(here > at + 1, (second - ratio * first) * over_d, 0.0)
            first = jnp.where(here > at, first * over_a, 0.0)

            def reduced(value):
                top, next_row = value[at : at + 1], value[at + 1 : at + 2]
                return value - first * top - low * (next_row - ratio * top)

            for k in range(at + 2, 8):
                columns[k] = reduced(columns[k])
            m = reduced(m)
    m = jnp.concatenate(done + [m], axis=0)
    pivots = jnp.sum(jnp.where(lane_pos == row_pos, m, 0.0), axis=1, keepdims=True)
    m = m * lax.rsqrt(pivots)
    upper = jnp.where(lane_pos >= row_pos, m, 0.0)[:, :n]
    return upper, m[:, 64 : 64 + n]


def eye(n):
    return (
        lax.broadcasted_iota(jnp.int32, (n, n), 0) == lax.broadcasted_iota(jnp.int32, (n, n), 1)
    ).astype(jnp.float32)


def factor_panels(total, width, work):
    count = total.shape[0] // width
    panels = [total[k * width :, k * width : (k + 1) * width] for k in range(count)]
    result = []
    for k in range(count):
        upper, inverse = factor_block(panels[k][:width], work)
        below = None
        if k + 1 < count:
            below = mm32(panels[k][width:], inverse, NT)
            for j in range(k + 1, count):
                at = (j - k - 1) * width
                panels[j] = panels[j] - mm32(below[at:], below[at : at + width], NT)
        result.append((upper, inverse, below))
    return result


def kernel(cube, panel, width, per_slot, leaves, geometry, *refs):
    refs = list(refs)
    take = lambda count: [refs.pop(0) for _ in range(count)]
    labels, columns = take(2)
    inv_hbm = dict(zip(LEVELS, take(4)))
    coup_hbm = dict(zip(LEVELS[:3], take(3)))
    gram_out, pick_out = take(2)
    proj_out = dict(zip(LEVELS, take(4)))
    inv = dict(zip(LEVELS, take(4)))
    coup = dict(zip(LEVELS[:3], take(3)))
    packed, arrived, place, places = take(4)
    tops = dict(zip(LEVELS[:3], take(3)))
    parts = take(1)[0]
    rest = dict(zip(LEVELS[:3], take(3)))
    linv = dict(zip(LEVELS[1:], take(3)))
    all_linv = dict(zip(LEVELS[:3], take(3)))
    all_tops = dict(zip(LEVELS[:3], take(3)))
    twin_sent = dict(zip(LEVELS, take(4)))
    twin_got = dict(zip(LEVELS, take(4)))
    sent = dict(zip(LEVELS, take(4)))
    got = dict(zip(LEVELS, take(4)))
    full = dict(zip(LEVELS, take(4)))
    gram = dict(zip(LEVELS, take(4)))
    gram_part = dict(zip(LEVELS, take(4)))
    cross = dict(zip(LEVELS[:3], take(3)))
    cross_part = dict(zip(LEVELS[:3], take(3)))
    work = take(1)[0]
    load_sem, route_send, route_recv, place_send, place_recv, panel_send, panel_recv, cube_send, cube_recv = take(9)

    c = lax.axis_index("cube")
    p = lax.axis_index("panel")
    chips = panel // 2
    chip, core = lax.div(p, 2), lax.rem(p, 2)

    def across(d):
        to, unit = chip, 1
        while unit < chips:
            if d // unit % 2:
                to = to + unit - 2 * unit * lax.rem(lax.div(chip, unit), 2)
            unit *= 2
        return to

    loads = {}
    for at, level in enumerate(LEVELS):
        loads[level, 0] = pltpu.make_async_copy(inv_hbm[level], inv[level], load_sem.at[at, 0])
    for at, level in ((1, 2), (2, 1)):
        loads[level, 1] = pltpu.make_async_copy(coup_hbm[level], coup[level], load_sem.at[at, 1])
    for j in range(3):
        loads[3, 1 + j] = pltpu.make_async_copy(
            coup_hbm[3].at[j], coup[3].at[j], load_sem.at[0, 1 + j]
        )
    loads[3, 0].start()

    barrier = pltpu.get_barrier_semaphore()

    def greet(axis, me, size):
        def one(d, carry):
            pl.semaphore_signal(
                barrier, inc=1, device_id={axis: lax.rem(me + d, size)}, device_id_type=MESH
            )
            return carry

        lax.fori_loop(1, size, one, 0)

    greet("cube", c, cube)
    greet("panel", p, panel)

    def greet_across(d, carry):
        pl.semaphore_signal(
            barrier, inc=1, device_id=(lax.rem(c + d, cube), p + 1 - 2 * core), device_id_type=MESH
        )
        return carry

    lax.fori_loop(1, cube, greet_across, 0)

    label = labels[...]
    time_cols = label.shape[1]
    share = cube // leaves
    onehot = lax.broadcasted_iota(jnp.int32, (16, time_cols), 0) == label
    earlier = lax.broadcasted_iota(jnp.int32, (time_cols, time_cols), 0) < (
        lax.broadcasted_iota(jnp.int32, (time_cols, time_cols), 1)
    )
    onehot = onehot.astype(jnp.float32)
    before = mm(onehot.astype(jnp.bfloat16), earlier.astype(jnp.float32).astype(jnp.bfloat16), NN)
    within = jnp.sum(before * onehot, axis=0, keepdims=True).astype(jnp.int32)
    turn = jnp.zeros_like(within)
    for step in range(1, share):
        turn = turn + (within >= step * per_slot).astype(jnp.int32)
    target = (label * share + turn) * (4 * SLOT) + within - turn * per_slot
    slot = (label * share + turn) * width + c * per_slot + within - turn * per_slot
    place[...] = jnp.zeros(place.shape, jnp.int32)
    place[:1, :time_cols] = slot
    stretch = (
        lax.broadcasted_iota(jnp.int32, (time_cols, 4 * time_cols), 0)
        == lax.div(lax.broadcasted_iota(jnp.int32, (time_cols, 4 * time_cols), 1), 4)
    ).astype(jnp.float32)
    sent_to = jnp.broadcast_to(target.astype(jnp.float32), (8, time_cols))
    sent_to = mm32(sent_to, stretch, NN)[:1] + 0.5
    kind_at = lax.rem(lax.broadcasted_iota(jnp.int32, (1, 4 * time_cols), 1), 4)
    sent_to = sent_to.astype(jnp.int32) + kind_at * SLOT
    dispatch = (
        (lax.broadcasted_iota(jnp.int32, (cube * 4 * SLOT, 4 * time_cols), 0) == sent_to)
        .astype(jnp.float32)
        .astype(jnp.bfloat16)
    )
    stripe = columns.shape[2]
    by_time = columns[...].reshape(4 * time_cols, stripe)
    packed[...] = mm(dispatch, by_time, NN).astype(jnp.bfloat16).reshape(cube, 4, SLOT, stripe)

    pl.semaphore_wait(barrier, 2 * cube + panel - 3)
    for load in ((3, 1), (2, 0), (3, 2), (3, 3), (2, 1), (1, 0), (1, 1), (0, 0)):
        loads[load].start()

    def route(d, rest):
        to = lax.rem(c + d, cube)
        blocks = pl.ds(1, 3) if rest else pl.ds(0, 1)
        return pltpu.make_async_remote_copy(
            src_ref=packed.at[to, blocks],
            dst_ref=arrived.at[c, blocks],
            send_sem=route_send.at[rest, d],
            recv_sem=route_recv.at[rest, d],
            device_id={"cube": to},
            device_id_type=MESH,
        )

    def each(low, high, do):
        def one(d, carry):
            do(d)
            return carry

        lax.fori_loop(low, high, one, 0)

    def tell(d):
        return pltpu.make_async_remote_copy(
            src_ref=place,
            dst_ref=places.at[c],
            send_sem=place_send.at[d],
            recv_sem=place_recv.at[d],
            device_id={"cube": lax.rem(c + d, cube)},
            device_id_type=MESH,
        )

    each(1, cube, lambda d: route(d, 0).start())
    each(1, cube, lambda d: route(d, 1).start())
    each(1, cube, lambda d: tell(d).start())
    arrived[c] = packed[c]
    places[c] = place[...]
    each(1, cube, lambda d: route(d, 0).wait_recv())
    out_pos = lax.broadcasted_iota(jnp.int32, (width, cube * SLOT), 0)
    in_pos = lax.broadcasted_iota(jnp.int32, (width, cube * SLOT), 1)
    select = jnp.zeros((width, cube * SLOT), jnp.float32)
    for s in range(cube):
        hit = (in_pos - s * SLOT == out_pos - s * per_slot) & (out_pos >= s * per_slot)
        hit = hit & (out_pos < (s + 1) * per_slot)
        select = select + hit.astype(jnp.float32)
    select = select.astype(jnp.bfloat16)
    first_size = geometry[3][0]
    pending = []

    def settle_block(j):
        mine = mm(select, arrived[:, j].reshape(cube * SLOT, stripe), NN)
        return mine.astype(jnp.bfloat16)

    def compact():
        each(1, cube, lambda d: tell(d).wait_recv())
        wide = cube * width
        slot_pos = lax.broadcasted_iota(jnp.int32, (wide, time_cols), 0)
        ones = jnp.ones((8, time_cols), jnp.bfloat16)
        used = jnp.zeros((8, wide), jnp.float32)
        for s in range(cube):
            at_slot = (slot_pos == places[s, :1, :time_cols]).astype(jnp.float32)
            used = used + mm(ones, at_slot.astype(jnp.bfloat16), NT)
        ahead = lax.broadcasted_iota(jnp.int32, (wide, wide), 0) < (
            lax.broadcasted_iota(jnp.int32, (wide, wide), 1)
        )
        count = mm(used.astype(jnp.bfloat16), ahead.astype(jnp.float32).astype(jnp.bfloat16), NN)
        row = lax.broadcasted_iota(jnp.int32, (cube * time_cols, wide), 0)
        hit = (row == count[:1].astype(jnp.int32)) & (used[:1] > 0.5)
        return hit.astype(jnp.float32)

    def interleave(chunk):
        step = min(128, chunk.shape[1])
        lane_in = lax.broadcasted_iota(jnp.int32, (step, 4 * step), 0)
        lane_out = lax.broadcasted_iota(jnp.int32, (step, 4 * step), 1)
        turned = jnp.where(lane_out < 2 * step, lane_out, lane_out - 2 * step - 1)
        expand = (turned == 2 * lane_in).astype(jnp.float32).astype(jnp.bfloat16)
        halves = []
        for at in range(0, chunk.shape[1], step):
            both = mm(chunk[:, at : at + step], expand, NN).astype(jnp.bfloat16)
            halves.append(jnp.concatenate([both[:, : 2 * step], both[:, 2 * step :]], axis=0))
        return jnp.concatenate(halves, axis=1)

    def fold(slots, stage, radix):
        value = slots[stage, 0].astype(jnp.float32)
        for s in range(1, radix):
            value = value + slots[stage, s].astype(jnp.float32)
        return value

    def group_copy(level, phase, block, d):
        size = geometry[level][0]
        rank = lax.rem(c, size)
        return pltpu.make_async_remote_copy(
            src_ref=block,
            dst_ref=block,
            send_sem=cube_send.at[level, phase, d],
            recv_sem=cube_recv.at[level, phase, d],
            device_id={"cube": c - rank + lax.rem(rank + d, size)},
            device_id_type=MESH,
        )

    shared = {}

    def share(level, phase, block):
        size = geometry[level][0]
        copy = lambda d: group_copy(level, phase, block, d)
        each(1, size, lambda d: copy(d).start())
        pending.append((1, size, copy))
        shared[level, phase] = copy

    def shared_wait(level, phase):
        copy = shared[level, phase]
        each(1, geometry[level][0], lambda d: copy(d).wait_recv())

    def sum_plan(level, kind, slots, acc):
        size = geometry[level][0]
        rank = lax.rem(c, size)
        stride = 1
        plan = []
        for stage, radix in enumerate(radices(size)):
            digit = lax.rem(lax.div(rank, stride), radix)

            def copy(d, stage=stage, digit=digit, stride=stride, radix=radix):
                return pltpu.make_async_remote_copy(
                    src_ref=slots.at[stage, digit],
                    dst_ref=slots.at[stage, digit],
                    send_sem=cube_send.at[level, 1 + 2 * stage + kind, d],
                    recv_sem=cube_recv.at[level, 1 + 2 * stage + kind, d],
                    device_id=(
                        c + (lax.rem(digit + d, radix) - digit) * stride,
                        p if kind else p + 1 - 2 * core,
                    ),
                    device_id_type=MESH,
                )

            def send(stage=stage, digit=digit, radix=radix, copy=copy):
                slots[stage, digit] = acc[...].astype(slots.dtype)
                each(1, radix, lambda d: copy(d).start())
                pending.append((1, radix, copy))

            def receive(stage=stage, radix=radix, copy=copy):
                each(1, radix, lambda d: copy(d).wait_recv())
                acc[...] = fold(slots, stage, radix)

            plan += [send, receive]
            stride = stride * radix
        return plan

    def run_all(plan):
        for step in plan:
            step()

    def own_rows(level, rows, store):
        if geometry[level][0] == 1:
            return rows
        store[...] = rows.reshape(store.shape).astype(store.dtype)
        return store[lax.rem(c, geometry[level][0])]

    def chunks(level):
        return [full[level][z, k] for z in range(panel // 2) for k in range(2)]

    def other_cross(level):
        part = geometry[level][2]
        if level == 3:
            for j in range(1, 3):
                loads[3, 1 + j].wait()
                value = None
                for at, chunk in enumerate(chunks(3)):
                    term = mm(chunk, coup[3][j, at * part : (at + 1) * part, :], NN)
                    value = term if value is None else value + term
                cross[3][j] = value

    def sum_chunks(level):
        value = None
        for chunk in chunks(level):
            term = mm(chunk, chunk, NT)
            value = term if value is None else value + term
        gram[level][...] = value

    def close(level, plan):
        size = geometry[level][0]
        wide = size * width
        if size == 1:
            sum_chunks(level)
        run_all(plan)
        blocks = factor_panels(eye(wide) + gram[level][...], width, work)
        rows = []
        for k, (_, inverse, _) in enumerate(blocks):
            right = None
            for e in range(k):
                at_row = (k - e - 1) * width
                term = mm32(blocks[e][2][at_row : at_row + width], rows[e], NN)
                right = term if right is None else right + term
            here = (
                lax.broadcasted_iota(jnp.int32, (width, wide), 1)
                == lax.broadcasted_iota(jnp.int32, (width, wide), 0) + k * width
            ).astype(jnp.float32)
            rows.append(mm32(inverse, here if right is None else here - right, NN))
        mine = own_rows(level, jnp.concatenate(rows, axis=0), all_linv[level])
        after = geometry[level - 1][0]
        at = lax.rem(c, after)
        linv[level - 1][at] = mine
        share(level - 1, 5, linv[level - 1].at[at])
        if size == 1:
            other_cross(level)
        for j in range(1, level):
            right = rest[level][:, j].reshape(wide, stripe).astype(jnp.float32) - cross[level][j]
            rest[level - 1][at, j - 1] = mm32(mine, right, NN).astype(jnp.bfloat16)
        if level > 1:
            share(level - 1, 6, rest[level - 1].at[at])

    def open_rest():
        each(1, cube, lambda d: route(d, 1).wait_recv())
        at = lax.rem(c, first_size)
        for j in range(3):
            rest[3][at, j] = settle_block(j + 1)
        share(3, 6, rest[3].at[at])
        pick_out[...] = compact()

    tops[3][lax.rem(c, first_size)] = settle_block(0)
    share(3, 0, tops[3].at[lax.rem(c, first_size)])
    later = open_rest

    for at, level in enumerate(LEVELS):
        size, rows, part = geometry[level]
        if size > 1:
            later()
            later = None
        shared_wait(level, 0)
        if level:
            wide = size * width
            top = tops[level][...].reshape(wide, stripe)
        else:
            pick = pick_out[...]
            below = geometry[1][0] * width
            sides = [
                pick[:, g * below : (g + 1) * below] for g in range(cube // geometry[1][0])
            ]
            top = None
            for s in range(cube):
                value = mm(sides[s // geometry[1][0]].astype(jnp.bfloat16), parts[s], NN)
                top = value if top is None else top + value
            top = top.astype(jnp.bfloat16)
            wide = top.shape[0]
        loads[level, 0].wait()

        def term(z, core, level=level, part=part, top=top):
            at_row = pl.multiple_of((2 * z + core) * part, part)
            return mm(top, inv[level][pl.ds(at_row, part), :], NT)

        def panel_copy(kind, src, dst, d, z, core, level=level):
            return pltpu.make_async_remote_copy(
                src_ref=src,
                dst_ref=dst,
                send_sem=panel_send.at[level, kind, d],
                recv_sem=panel_recv.at[level, kind, d],
                device_id={"panel": 2 * z + core},
                device_id_type=MESH,
            )

        def to_twin(d, level=level, panel_copy=panel_copy):
            return panel_copy(0, twin_sent[level].at[d], twin_got[level].at[d], d, chip, 1 - core)

        def scatter(d, level=level, panel_copy=panel_copy):
            to = across(d)
            return panel_copy(1, sent[level].at[d], got[level].at[d], d, to, 1 - core)

        def send_twin(d, side, level=level, term=term, to_twin=to_twin):
            twin_sent[level][d] = term(across(d), side).astype(jnp.bfloat16)
            to_twin(d).start()

        def send_term(d, level=level, term=term, to_twin=to_twin, scatter=scatter):
            mine = term(across(d), 1 - core)
            to_twin(d).wait_recv()
            sent[level][d] = (mine + twin_got[level][d].astype(jnp.float32)).astype(jnp.bfloat16)
            scatter(d).start()

        for d in range(chips - 1, 0, -1):
            send_twin(d, core)
        send_twin(0, 1 - core)
        for d in range(chips - 1, 0, -1):
            send_term(d)
        own = term(chip, core)
        if later is not None:
            later()
        to_twin(0).wait_recv()
        own = own + twin_got[level][0].astype(jnp.float32)
        if level < 3:
            shared_wait(level, 5)
            child = geometry[level + 1][0]
            inner = child * width
            nodes = size // child
            lower = [
                linv[level][n * child : (n + 1) * child].reshape(inner, inner)
                for n in range(nodes)
            ]
            if not level:
                scale = None
                for n in range(nodes):
                    value = mm32(sides[n], mm32(lower[n], sides[n], NT), NN)
                    scale = value if scale is None else scale + value
        for d in range(1, chips):
            scatter(d).wait_recv()
            own = own + got[level][d].astype(jnp.float32)
        if not level:
            own = mm32(scale, own, NN)
        elif level < 3:
            own = jnp.concatenate(
                [mm32(lower[n], own[n * inner : (n + 1) * inner], NN) for n in range(nodes)], axis=0
            )
        own = own.astype(jnp.bfloat16)
        full[level][chip, core] = own

        def gather(d, level=level, panel_copy=panel_copy):
            here = full[level].at[chip, core]
            return panel_copy(2, here, here, d, across(d), 1 - core)

        def forward(d, side, level=level, panel_copy=panel_copy):
            here = full[level].at[across(d), side]
            return panel_copy(3, here, here, d, chip, 1 - core)

        for d in range(chips - 1, 0, -1):
            gather(d).start()
        forward(0, core).start()
        proj_out[level][...] = own
        pending.append((0, chips, to_twin))
        pending.append((1, chips, scatter))
        pending.append((1, chips, gather))
        pending.append((0, 1, lambda d, forward=forward: forward(d, core)))
        pending.append((1, chips, lambda d, forward=forward: forward(d, 1 - core)))

        if level:
            loads[level, 1].wait()

        def add_chunk(z, core, first, level=level, part=part, wide=wide):
            chunk = full[level][z, core]
            at_row = pl.multiple_of((2 * z + core) * part, part)
            if not level:
                value = mm(chunk, chunk, NT)
                gram[0][...] = value if first else gram[0][...] + value
            elif level == 2:
                value = mm(interleave(chunk), coup[2][pl.ds(at_row, part)].reshape(2 * part, stripe), NN)
                value = value.reshape(2, wide, stripe)
                cross[2][...] = value if first else cross[2][...] + value
            else:
                value = mm(chunk, coup[level][0, pl.ds(at_row, part), :], NN)
                cross[level][0] = value if first else cross[level][0] + value
                if level == 1:
                    value = mm(chunk, chunk, NT)
                    gram[1][...] = value if first else gram[1][...] + value

        add_chunk(chip, core, True)

        def receive(d, gather=gather, forward=forward, add_chunk=add_chunk):
            gather(d).wait_recv()
            forward(d, 1 - core).start()
            add_chunk(across(d), 1 - core, False)

        def receive_twin(d, side, forward=forward, add_chunk=add_chunk):
            forward(d, 1 - side).wait_recv()
            add_chunk(across(d), side, False)

        receive_twin(0, 1 - core)
        for d in range(1, chips):
            receive(d)
        for d in range(1, chips):
            receive_twin(d, core)

        if not level:
            run_all(sum_plan(0, 0, gram_part[0], gram[0]))
            gram_out[...] = eye(wide) + gram[0][...]
            break
        plan = sum_plan(level, 0, gram_part[level], gram[level])
        if size > 1:
            if level > 1:
                sum_chunks(level)
            plan[0]()
        shared_wait(level, 6)
        if level > 1 and size > 1:
            other_cross(level)
            run_all(sum_plan(level, 1, cross_part[level], cross[level]))
        right = rest[level][:, 0].reshape(wide, stripe).astype(jnp.float32)
        after = geometry[level - 1][0]
        at = lax.rem(c, after)
        if level > 1:
            right = (right - cross[level][0]).astype(jnp.bfloat16)
            tops[level - 1][at] = own_rows(level, right, all_tops[level])
            share(level - 1, 0, tops[level - 1].at[at])
        else:
            right = jnp.where(lax.rem(c, size) == 0, right, 0.0) - cross[1][0]
            parts[at] = right.astype(jnp.bfloat16)
            share(0, 0, parts.at[at])
        later = functools.partial(close, level, plan[1:])

    for block in (0, 1):
        each(1, cube, lambda d, block=block: route(d, block).wait_send())
    each(1, cube, lambda d: tell(d).wait_send())
    for low, high, copy in pending:
        for d in range(low, high):
            copy(d).wait_send()


def finish(width, total, pick, root, leaf, middle, upper, core_out, root_out, *refs):
    results, (work, low_factor, sems) = refs[:3], refs[3:]
    copies = [
        pltpu.make_async_copy(source, result, sems.at[k])
        for k, (source, result) in enumerate(zip((leaf, middle, upper), results))
    ]
    for copy in copies:
        copy.start()
    chosen = pick[...]
    wide, slots = chosen.shape
    low_factor[...] = jnp.zeros(low_factor.shape, jnp.float32)
    for k, (upper_part, _, below) in enumerate(factor_panels(total[...], width, work)):
        low = k * width
        low_factor[low : low + width, low : low + width] = mm32(eye(width), upper_part, NT)
        if below is not None:
            low_factor[low + width :, low : low + width] = below
    spread = mm32(low_factor[...], chosen, NN)
    narrow = chosen.astype(jnp.bfloat16)
    used = mm(narrow, jnp.ones((wide, slots), jnp.bfloat16), TN)
    core_out[...] = mm32(chosen, spread, TN) + eye(slots) * (1.0 - used)
    root_out[...] = mm(narrow, root[...], TN).astype(jnp.bfloat16)
    for copy in copies:
        copy.wait()


def body(
    cube,
    panel,
    columns,
    leaf_of,
    inverse_root,
    inverse_upper,
    inverse_middle,
    inverse_leaf,
    coupling_upper,
    coupling_middle,
    coupling_leaf,
):
    time_cols, _, stripe = columns.shape
    leaves = min(8, cube)
    leaf_share = cube // leaves
    per_slot = max(1, (2 * time_cols // leaves + leaf_share - 1) // leaf_share)
    width = cube * per_slot
    inverses = [inverse_leaf, inverse_middle, inverse_upper, inverse_root]
    couplings = [
        jnp.transpose(coupling_leaf, (1, 0, 2)),
        coupling_middle,
        jnp.transpose(coupling_upper, (1, 0, 2)),
    ]
    geometry = {}
    for level, inverse in zip(LEVELS, inverses):
        rows = inverse.shape[0]
        geometry[level] = (cube // min(2**level, cube), rows, rows // panel)
    wide = {level: geometry[level][0] * width for level in LEVELS}
    ranks = cube * time_cols
    slots = wide[0]
    wide[0] = ranks
    part = {level: geometry[level][2] for level in LEVELS}
    size = {level: geometry[level][0] for level in LEVELS}
    vm = pltpu.VMEM
    scratch = [vm(x.shape, x.dtype) for x in inverses]
    scratch += [vm(x.shape, x.dtype) for x in couplings]
    scratch += [vm((cube, 4, SLOT, stripe), jnp.bfloat16)] * 2
    scratch += [vm((8, 128), jnp.int32), vm((cube, 8, 128), jnp.int32)]
    scratch += [vm((size[l], width, stripe), jnp.bfloat16) for l in LEVELS[:3]]
    scratch += [vm((cube, wide[1], stripe), jnp.bfloat16)]
    scratch += [vm((size[l], l, width, stripe), jnp.bfloat16) for l in LEVELS[:3]]
    scratch += [vm((size[l], width, wide[l + 1]), jnp.float32) for l in LEVELS[1:]]
    scratch += [vm((size[l], width, wide[l]), jnp.float32) for l in LEVELS[:3]]
    scratch += [vm((size[l], width, stripe), jnp.bfloat16) for l in LEVELS[:3]]
    for _ in range(4):
        scratch += [vm((panel // 2, wide[l], part[l]), jnp.bfloat16) for l in LEVELS]
    scratch += [vm((panel // 2, 2, wide[l], part[l]), jnp.bfloat16) for l in LEVELS]
    scratch += [vm((wide[l], wide[l]), jnp.float32) for l in LEVELS]
    for l in LEVELS:
        steps = radices(size[l]) or [1]
        kind = jnp.float32 if size[l] <= 2 else jnp.bfloat16
        scratch += [vm((len(steps), max(steps), wide[l], wide[l]) if size[l] > 1 else (1, 1, 8, 128), kind)]
    scratch += [vm((l, wide[l], stripe), jnp.float32) for l in LEVELS[:3]]
    for l in LEVELS[:3]:
        steps = radices(size[l]) or [1]
        used = l > 1 and size[l] > 1
        scratch += [vm((len(steps), max(steps), l, wide[l], stripe) if used else (1, 1, 1, 16, 128), jnp.bfloat16)]
    scratch += [vm((width, 128), jnp.float32)]
    dma = pltpu.SemaphoreType.DMA
    scratch += [dma((4, 4)), dma((2, cube)), dma((2, cube)), dma((cube,)), dma((cube,)), dma((4, 4, panel // 2)), dma((4, 4, panel // 2))]
    scratch += [dma((4, 7, cube)), dma((4, 7, cube))]
    shape = jax.ShapeDtypeStruct
    passed = [shape((wide[l], part[l]), jnp.bfloat16) for l in LEVELS]
    outs = [shape((ranks, ranks), jnp.float32), shape((ranks, slots), jnp.float32)] + passed
    in_vmem = pl.BlockSpec(memory_space=pltpu.VMEM)
    in_any = pl.BlockSpec(memory_space=pl.ANY)
    total, pick, leaf, middle, upper, root = pl.pallas_call(
        functools.partial(kernel, cube, panel, width, per_slot, leaves, geometry),
        out_shape=outs,
        in_specs=[in_vmem, in_vmem] + [in_any] * 7,
        out_specs=[in_vmem] * 6,
        scratch_shapes=scratch,
        compiler_params=pltpu.CompilerParams(
            collective_id=0, has_side_effects=True, vmem_limit_bytes=58 * 2**20
        ),
    )(
        jnp.transpose(leaf_of),
        columns,
        *inverses,
        *couplings,
    )
    core, root, leaf, middle, upper = pl.pallas_call(
        functools.partial(finish, width),
        out_shape=[shape((slots, slots), jnp.float32), shape((slots, part[0]), jnp.bfloat16)]
        + passed[:3],
        in_specs=[in_vmem] * 6,
        out_specs=[in_vmem] * 2 + [in_any] * 3,
        scratch_shapes=[vm((width, 128), jnp.float32), vm((ranks, ranks), jnp.float32), dma((3,))],
    )(total, pick, root, leaf, middle, upper)
    return (core, root.T, upper.T, middle.T, leaf.T)


def solution(mesh):
    in_specs = (
        P("cube", None, "panel"),
        P("cube", None),
        P("cube", "panel"),
        P("cube", "panel"),
        P("cube", "panel"),
        P("cube", "panel"),
        P("cube", None, "panel"),
        P("cube", None, "panel"),
        P("cube", None, "panel"),
    )
    out_specs = (
        P(),
        P(("cube", "panel"), None),
        P(("cube", "panel"), None),
        P(("cube", "panel"), None),
        P(("cube", "panel"), None),
    )
    run = functools.partial(body, mesh.shape["cube"], mesh.shape["panel"])
    return jax.shard_map(run, mesh=mesh, in_specs=in_specs, out_specs=out_specs, check_vma=False)
```

```python
import functools

import jax
import jax.numpy as jnp
from jax import lax
from jax.experimental import pallas as pl
from jax.experimental.pallas import tpu as pltpu
from jax.sharding import PartitionSpec as P

MESH = pl.DeviceIdType.MESH
LEVELS = (3, 2, 1, 0)
SLOT = 16
NT = (((1,), (1,)), ((), ()))
NN = (((1,), (0,)), ((), ()))
TN = (((0,), (0,)), ((), ()))


def radices(size):
    steps = []
    while size > 1:
        steps.append(min(4, size))
        size //= steps[-1]
    return steps


def mm(a, b, dims):
    return lax.dot_general(a, b, dims, preferred_element_type=jnp.float32)


def mm32(a, b, dims):
    return lax.dot_general(
        a, b, dims, precision=lax.Precision.HIGHEST, preferred_element_type=jnp.float32
    )


def factor_block(block, work):
    n = block.shape[0]
    work[:, :n] = block
    row_pos = lax.broadcasted_iota(jnp.int32, (n, 128), 0)
    lane_pos = lax.broadcasted_iota(jnp.int32, (n, 128), 1)
    m = jnp.where(lane_pos < n, work[...], 0.0) + (lane_pos == row_pos + 64).astype(jnp.float32)
    done = []
    for base in range(0, n, 8):
        if base:
            done.append(m[:8])
            m = m[8:]
        shape = m.shape
        here = row_pos[: shape[0]]
        columns = [jnp.broadcast_to(m[:, base + at : base + at + 1], shape) for at in range(8)]
        for at in range(0, 8, 2):
            first, second = columns[at], columns[at + 1]
            a, b, d = first[at : at + 1], first[at + 1 : at + 2], second[at + 1 : at + 2]
            over_a, over_d = 1.0 / a, a * (1.0 / (a * d - b * b))
            ratio = b * over_a
            low = jnp.where(here > at + 1, (second - ratio * first) * over_d, 0.0)
            first = jnp.where(here > at, first * over_a, 0.0)

            def reduced(value):
                top, next_row = value[at : at + 1], value[at + 1 : at + 2]
                return value - first * top - low * (next_row - ratio * top)

            for k in range(at + 2, 8):
                columns[k] = reduced(columns[k])
            m = reduced(m)
    m = jnp.concatenate(done + [m], axis=0)
    pivots = jnp.sum(jnp.where(lane_pos == row_pos, m, 0.0), axis=1, keepdims=True)
    m = m * lax.rsqrt(pivots)
    upper = jnp.where(lane_pos >= row_pos, m, 0.0)[:, :n]
    return upper, m[:, 64 : 64 + n]


def eye(n):
    return (
        lax.broadcasted_iota(jnp.int32, (n, n), 0) == lax.broadcasted_iota(jnp.int32, (n, n), 1)
    ).astype(jnp.float32)


def factor_panels(total, width, work):
    count = total.shape[0] // width
    panels = [total[k * width :, k * width : (k + 1) * width] for k in range(count)]
    result = []
    for k in range(count):
        upper, inverse = factor_block(panels[k][:width], work)
        below = None
        if k + 1 < count:
            below = mm32(panels[k][width:], inverse, NT)
            for j in range(k + 1, count):
                at = (j - k - 1) * width
                panels[j] = panels[j] - mm32(below[at:], below[at : at + width], NT)
        result.append((upper, inverse, below))
    return result


def kernel(cube, panel, width, per_slot, leaves, geometry, *refs):
    refs = list(refs)
    take = lambda count: [refs.pop(0) for _ in range(count)]
    labels, columns = take(2)
    inv_hbm = dict(zip(LEVELS, take(4)))
    coup_hbm = dict(zip(LEVELS[:3], take(3)))
    gram_out, pick_out = take(2)
    proj_out = dict(zip(LEVELS, take(4)))
    inv = dict(zip(LEVELS, take(4)))
    coup = dict(zip(LEVELS[:3], take(3)))
    packed, arrived, place, places = take(4)
    tops = dict(zip(LEVELS[:3], take(3)))
    parts = take(1)[0]
    rest = dict(zip(LEVELS[:3], take(3)))
    linv = dict(zip(LEVELS[1:], take(3)))
    all_linv = dict(zip(LEVELS[:3], take(3)))
    all_tops = dict(zip(LEVELS[:3], take(3)))
    twin_sent = dict(zip(LEVELS, take(4)))
    twin_got = dict(zip(LEVELS, take(4)))
    sent = dict(zip(LEVELS, take(4)))
    got = dict(zip(LEVELS, take(4)))
    full = dict(zip(LEVELS, take(4)))
    gram = dict(zip(LEVELS, take(4)))
    gram_part = dict(zip(LEVELS, take(4)))
    cross = dict(zip(LEVELS[:3], take(3)))
    cross_part = dict(zip(LEVELS[:3], take(3)))
    work = take(1)[0]
    load_sem, route_send, route_recv, place_send, place_recv, panel_send, panel_recv, cube_send, cube_recv = take(9)

    c = lax.axis_index("cube")
    p = lax.axis_index("panel")
    chips = panel // 2
    chip, core = lax.div(p, 2), lax.rem(p, 2)

    def across(d):
        to, unit = chip, 1
        while unit < chips:
            if d // unit % 2:
                to = to + unit - 2 * unit * lax.rem(lax.div(chip, unit), 2)
            unit *= 2
        return to

    loads = {}
    for at, level in enumerate(LEVELS):
        loads[level, 0] = pltpu.make_async_copy(inv_hbm[level], inv[level], load_sem.at[at, 0])
    for at, level in ((1, 2), (2, 1)):
        loads[level, 1] = pltpu.make_async_copy(coup_hbm[level], coup[level], load_sem.at[at, 1])
    for j in range(3):
        loads[3, 1 + j] = pltpu.make_async_copy(
            coup_hbm[3].at[j], coup[3].at[j], load_sem.at[0, 1 + j]
        )
    loads[3, 0].start()

    barrier = pltpu.get_barrier_semaphore()

    def greet(axis, me, size):
        def one(d, carry):
            pl.semaphore_signal(
                barrier, inc=1, device_id={axis: lax.rem(me + d, size)}, device_id_type=MESH
            )
            return carry

        lax.fori_loop(1, size, one, 0)

    greet("cube", c, cube)
    greet("panel", p, panel)

    def greet_across(d, carry):
        pl.semaphore_signal(
            barrier, inc=1, device_id=(lax.rem(c + d, cube), p + 1 - 2 * core), device_id_type=MESH
        )
        return carry

    lax.fori_loop(1, cube, greet_across, 0)

    label = labels[...]
    time_cols = label.shape[1]
    share = cube // leaves
    onehot = lax.broadcasted_iota(jnp.int32, (16, time_cols), 0) == label
    earlier = lax.broadcasted_iota(jnp.int32, (time_cols, time_cols), 0) < (
        lax.broadcasted_iota(jnp.int32, (time_cols, time_cols), 1)
    )
    onehot = onehot.astype(jnp.float32)
    before = mm(onehot.astype(jnp.bfloat16), earlier.astype(jnp.float32).astype(jnp.bfloat16), NN)
    within = jnp.sum(before * onehot, axis=0, keepdims=True).astype(jnp.int32)
    turn = jnp.zeros_like(within)
    for step in range(1, share):
        turn = turn + (within >= step * per_slot).astype(jnp.int32)
    target = (label * share + turn) * (4 * SLOT) + within - turn * per_slot
    slot = (label * share + turn) * width + c * per_slot + within - turn * per_slot
    place[...] = jnp.zeros(place.shape, jnp.int32)
    place[:1, :time_cols] = slot
    stretch = (
        lax.broadcasted_iota(jnp.int32, (time_cols, 4 * time_cols), 0)
        == lax.div(lax.broadcasted_iota(jnp.int32, (time_cols, 4 * time_cols), 1), 4)
    ).astype(jnp.float32)
    sent_to = jnp.broadcast_to(target.astype(jnp.float32), (8, time_cols))
    sent_to = mm32(sent_to, stretch, NN)[:1] + 0.5
    kind_at = lax.rem(lax.broadcasted_iota(jnp.int32, (1, 4 * time_cols), 1), 4)
    sent_to = sent_to.astype(jnp.int32) + kind_at * SLOT
    dispatch = (
        (lax.broadcasted_iota(jnp.int32, (cube * 4 * SLOT, 4 * time_cols), 0) == sent_to)
        .astype(jnp.float32)
        .astype(jnp.bfloat16)
    )
    stripe = columns.shape[2]
    by_time = columns[...].reshape(4 * time_cols, stripe)
    packed[...] = mm(dispatch, by_time, NN).astype(jnp.bfloat16).reshape(cube, 4, SLOT, stripe)

    pl.semaphore_wait(barrier, 2 * cube + panel - 3)
    for load in ((3, 1), (2, 0), (3, 2), (3, 3), (2, 1), (1, 0), (1, 1), (0, 0)):
        loads[load].start()

    def route(d, rest):
        to = lax.rem(c + d, cube)
        blocks = pl.ds(1, 3) if rest else pl.ds(0, 1)
        return pltpu.make_async_remote_copy(
            src_ref=packed.at[to, blocks],
            dst_ref=arrived.at[c, blocks],
            send_sem=route_send.at[rest, d],
            recv_sem=route_recv.at[rest, d],
            device_id={"cube": to},
            device_id_type=MESH,
        )

    def each(low, high, do):
        def one(d, carry):
            do(d)
            return carry

        lax.fori_loop(low, high, one, 0)

    def tell(d):
        return pltpu.make_async_remote_copy(
            src_ref=place,
            dst_ref=places.at[c],
            send_sem=place_send.at[d],
            recv_sem=place_recv.at[d],
            device_id={"cube": lax.rem(c + d, cube)},
            device_id_type=MESH,
        )

    each(1, cube, lambda d: route(d, 0).start())
    each(1, cube, lambda d: route(d, 1).start())
    each(1, cube, lambda d: tell(d).start())
    arrived[c] = packed[c]
    places[c] = place[...]
    each(1, cube, lambda d: route(d, 0).wait_recv())
    out_pos = lax.broadcasted_iota(jnp.int32, (width, cube * SLOT), 0)
    in_pos = lax.broadcasted_iota(jnp.int32, (width, cube * SLOT), 1)
    select = jnp.zeros((width, cube * SLOT), jnp.float32)
    for s in range(cube):
        hit = (in_pos - s * SLOT == out_pos - s * per_slot) & (out_pos >= s * per_slot)
        hit = hit & (out_pos < (s + 1) * per_slot)
        select = select + hit.astype(jnp.float32)
    select = select.astype(jnp.bfloat16)
    first_size = geometry[3][0]
    pending = []

    def settle_block(j):
        mine = mm(select, arrived[:, j].reshape(cube * SLOT, stripe), NN)
        return mine.astype(jnp.bfloat16)

    def compact():
        each(1, cube, lambda d: tell(d).wait_recv())
        wide = cube * width
        slot_pos = lax.broadcasted_iota(jnp.int32, (wide, time_cols), 0)
        ones = jnp.ones((8, time_cols), jnp.bfloat16)
        used = jnp.zeros((8, wide), jnp.float32)
        for s in range(cube):
            at_slot = (slot_pos == places[s, :1, :time_cols]).astype(jnp.float32)
            used = used + mm(ones, at_slot.astype(jnp.bfloat16), NT)
        ahead = lax.broadcasted_iota(jnp.int32, (wide, wide), 0) < (
            lax.broadcasted_iota(jnp.int32, (wide, wide), 1)
        )
        count = mm(used.astype(jnp.bfloat16), ahead.astype(jnp.float32).astype(jnp.bfloat16), NN)
        row = lax.broadcasted_iota(jnp.int32, (cube * time_cols, wide), 0)
        hit = (row == count[:1].astype(jnp.int32)) & (used[:1] > 0.5)
        return hit.astype(jnp.float32)

    def interleave(chunk):
        step = min(128, chunk.shape[1])
        lane_in = lax.broadcasted_iota(jnp.int32, (step, 4 * step), 0)
        lane_out = lax.broadcasted_iota(jnp.int32, (step, 4 * step), 1)
        turned = jnp.where(lane_out < 2 * step, lane_out, lane_out - 2 * step - 1)
        expand = (turned == 2 * lane_in).astype(jnp.float32).astype(jnp.bfloat16)
        halves = []
        for at in range(0, chunk.shape[1], step):
            both = mm(chunk[:, at : at + step], expand, NN).astype(jnp.bfloat16)
            halves.append(jnp.concatenate([both[:, : 2 * step], both[:, 2 * step :]], axis=0))
        return jnp.concatenate(halves, axis=1)

    def fold(slots, stage, radix):
        value = slots[stage, 0].astype(jnp.float32)
        for s in range(1, radix):
            value = value + slots[stage, s].astype(jnp.float32)
        return value

    def group_copy(level, phase, block, d):
        size = geometry[level][0]
        rank = lax.rem(c, size)
        return pltpu.make_async_remote_copy(
            src_ref=block,
            dst_ref=block,
            send_sem=cube_send.at[level, phase, d],
            recv_sem=cube_recv.at[level, phase, d],
            device_id={"cube": c - rank + lax.rem(rank + d, size)},
            device_id_type=MESH,
        )

    shared = {}

    def share(level, phase, block):
        size = geometry[level][0]
        copy = lambda d: group_copy(level, phase, block, d)
        each(1, size, lambda d: copy(d).start())
        pending.append((1, size, copy))
        shared[level, phase] = copy

    def shared_wait(level, phase):
        copy = shared[level, phase]
        each(1, geometry[level][0], lambda d: copy(d).wait_recv())

    def sum_plan(level, kind, slots, acc):
        size = geometry[level][0]
        rank = lax.rem(c, size)
        stride = 1
        plan = []
        for stage, radix in enumerate(radices(size)):
            digit = lax.rem(lax.div(rank, stride), radix)

            def copy(d, stage=stage, digit=digit, stride=stride, radix=radix):
                return pltpu.make_async_remote_copy(
                    src_ref=slots.at[stage, digit],
                    dst_ref=slots.at[stage, digit],
                    send_sem=cube_send.at[level, 1 + 2 * stage + kind, d],
                    recv_sem=cube_recv.at[level, 1 + 2 * stage + kind, d],
                    device_id=(
                        c + (lax.rem(digit + d, radix) - digit) * stride,
                        p if kind else p + 1 - 2 * core,
                    ),
                    device_id_type=MESH,
                )

            def send(stage=stage, digit=digit, radix=radix, copy=copy):
                slots[stage, digit] = acc[...].astype(slots.dtype)
                each(1, radix, lambda d: copy(d).start())
                pending.append((1, radix, copy))

            def receive(stage=stage, radix=radix, copy=copy):
                each(1, radix, lambda d: copy(d).wait_recv())
                acc[...] = fold(slots, stage, radix)

            plan += [send, receive]
            stride = stride * radix
        return plan

    def run_all(plan):
        for step in plan:
            step()

    def own_rows(level, rows, store):
        if geometry[level][0] == 1:
            return rows
        store[...] = rows.reshape(store.shape).astype(store.dtype)
        return store[lax.rem(c, geometry[level][0])]

    def chunks(level):
        return [full[level][z, k] for z in range(panel // 2) for k in range(2)]

    def other_cross(level):
        part = geometry[level][2]
        if level == 3:
            for j in range(1, 3):
                loads[3, 1 + j].wait()
                value = None
                for at, chunk in enumerate(chunks(3)):
                    term = mm(chunk, coup[3][j, at * part : (at + 1) * part, :], NN)
                    value = term if value is None else value + term
                cross[3][j] = value

    def sum_chunks(level):
        value = None
        for chunk in chunks(level):
            term = mm(chunk, chunk, NT)
            value = term if value is None else value + term
        gram[level][...] = value

    def close(level, plan):
        size = geometry[level][0]
        wide = size * width
        if size == 1:
            sum_chunks(level)
        run_all(plan)
        blocks = factor_panels(eye(wide) + gram[level][...], width, work)
        rows = []
        for k, (_, inverse, _) in enumerate(blocks):
            right = None
            for e in range(k):
                at_row = (k - e - 1) * width
                term = mm32(blocks[e][2][at_row : at_row + width], rows[e], NN)
                right = term if right is None else right + term
            here = (
                lax.broadcasted_iota(jnp.int32, (width, wide), 1)
                == lax.broadcasted_iota(jnp.int32, (width, wide), 0) + k * width
            ).astype(jnp.float32)
            rows.append(mm32(inverse, here if right is None else here - right, NN))
        mine = own_rows(level, jnp.concatenate(rows, axis=0), all_linv[level])
        after = geometry[level - 1][0]
        at = lax.rem(c, after)
        linv[level - 1][at] = mine
        share(level - 1, 5, linv[level - 1].at[at])

        def other_blocks():
            if size == 1:
                other_cross(level)
            for j in range(1, level):
                right = rest[level][:, j].reshape(wide, stripe).astype(jnp.float32)
                right = right - cross[level][j]
                rest[level - 1][at, j - 1] = mm32(mine, right, NN).astype(jnp.bfloat16)
            if level > 1:
                share(level - 1, 6, rest[level - 1].at[at])

        return other_blocks

    def open_rest():
        each(1, cube, lambda d: route(d, 1).wait_recv())
        at = lax.rem(c, first_size)
        for j in range(3):
            rest[3][at, j] = settle_block(j + 1)
        share(3, 6, rest[3].at[at])
        pick_out[...] = compact()
        return lambda: None

    tops[3][lax.rem(c, first_size)] = settle_block(0)
    share(3, 0, tops[3].at[lax.rem(c, first_size)])
    later = open_rest

    for at, level in enumerate(LEVELS):
        size, rows, part = geometry[level]
        if size > 1:
            others = later()
            later = None
        shared_wait(level, 0)
        if level:
            wide = size * width
            top = tops[level][...].reshape(wide, stripe)
        else:
            pick = pick_out[...]
            below = geometry[1][0] * width
            sides = [
                pick[:, g * below : (g + 1) * below] for g in range(cube // geometry[1][0])
            ]
            top = None
            for s in range(cube):
                value = mm(sides[s // geometry[1][0]].astype(jnp.bfloat16), parts[s], NN)
                top = value if top is None else top + value
            top = top.astype(jnp.bfloat16)
            wide = top.shape[0]
        loads[level, 0].wait()

        def term(z, core, level=level, part=part, top=top):
            at_row = pl.multiple_of((2 * z + core) * part, part)
            return mm(top, inv[level][pl.ds(at_row, part), :], NT)

        def panel_copy(kind, src, dst, d, z, core, level=level):
            return pltpu.make_async_remote_copy(
                src_ref=src,
                dst_ref=dst,
                send_sem=panel_send.at[level, kind, d],
                recv_sem=panel_recv.at[level, kind, d],
                device_id={"panel": 2 * z + core},
                device_id_type=MESH,
            )

        def to_twin(d, level=level, panel_copy=panel_copy):
            return panel_copy(0, twin_sent[level].at[d], twin_got[level].at[d], d, chip, 1 - core)

        def scatter(d, level=level, panel_copy=panel_copy):
            to = across(d)
            return panel_copy(1, sent[level].at[d], got[level].at[d], d, to, 1 - core)

        def send_twin(d, side, level=level, term=term, to_twin=to_twin):
            twin_sent[level][d] = term(across(d), side).astype(jnp.bfloat16)
            to_twin(d).start()

        def send_term(d, level=level, term=term, to_twin=to_twin, scatter=scatter):
            mine = term(across(d), 1 - core)
            to_twin(d).wait_recv()
            sent[level][d] = (mine + twin_got[level][d].astype(jnp.float32)).astype(jnp.bfloat16)
            scatter(d).start()

        for d in range(chips - 1, 0, -1):
            send_twin(d, core)
        send_twin(0, 1 - core)
        for d in range(chips - 1, 0, -1):
            send_term(d)
        own = term(chip, core)
        if later is not None:
            others = later()
        to_twin(0).wait_recv()
        own = own + twin_got[level][0].astype(jnp.float32)
        if level < 3:
            shared_wait(level, 5)
            child = geometry[level + 1][0]
            inner = child * width
            nodes = size // child
            lower = [
                linv[level][n * child : (n + 1) * child].reshape(inner, inner)
                for n in range(nodes)
            ]
            if not level:
                scale = None
                for n in range(nodes):
                    value = mm32(sides[n], mm32(lower[n], sides[n], NT), NN)
                    scale = value if scale is None else scale + value
        for d in range(1, chips):
            scatter(d).wait_recv()
            own = own + got[level][d].astype(jnp.float32)
        if not level:
            own = mm32(scale, own, NN)
        elif level < 3:
            own = jnp.concatenate(
                [mm32(lower[n], own[n * inner : (n + 1) * inner], NN) for n in range(nodes)], axis=0
            )
        own = own.astype(jnp.bfloat16)
        full[level][chip, core] = own

        def gather(d, level=level, panel_copy=panel_copy):
            here = full[level].at[chip, core]
            return panel_copy(2, here, here, d, across(d), 1 - core)

        def forward(d, side, level=level, panel_copy=panel_copy):
            here = full[level].at[across(d), side]
            return panel_copy(3, here, here, d, chip, 1 - core)

        for d in range(chips - 1, 0, -1):
            gather(d).start()
        forward(0, core).start()
        others()
        proj_out[level][...] = own
        pending.append((0, chips, to_twin))
        pending.append((1, chips, scatter))
        pending.append((1, chips, gather))
        pending.append((0, 1, lambda d, forward=forward: forward(d, core)))
        pending.append((1, chips, lambda d, forward=forward: forward(d, 1 - core)))

        if level:
            loads[level, 1].wait()

        def add_chunk(z, core, first, level=level, part=part, wide=wide):
            chunk = full[level][z, core]
            at_row = pl.multiple_of((2 * z + core) * part, part)
            if not level:
                value = mm(chunk, chunk, NT)
                gram[0][...] = value if first else gram[0][...] + value
            elif level == 2:
                value = mm(interleave(chunk), coup[2][pl.ds(at_row, part)].reshape(2 * part, stripe), NN)
                value = value.reshape(2, wide, stripe)
                cross[2][...] = value if first else cross[2][...] + value
            else:
                value = mm(chunk, coup[level][0, pl.ds(at_row, part), :], NN)
                cross[level][0] = value if first else cross[level][0] + value
                if level == 1:
                    value = mm(chunk, chunk, NT)
                    gram[1][...] = value if first else gram[1][...] + value

        add_chunk(chip, core, True)

        def receive(d, gather=gather, forward=forward, add_chunk=add_chunk):
            gather(d).wait_recv()
            forward(d, 1 - core).start()
            add_chunk(across(d), 1 - core, False)

        def receive_twin(d, side, forward=forward, add_chunk=add_chunk):
            forward(d, 1 - side).wait_recv()
            add_chunk(across(d), side, False)

        receive_twin(0, 1 - core)
        for d in range(1, chips):
            receive(d)
        for d in range(1, chips):
            receive_twin(d, core)

        if not level:
            run_all(sum_plan(0, 0, gram_part[0], gram[0]))
            gram_out[...] = eye(wide) + gram[0][...]
            break
        plan = sum_plan(level, 0, gram_part[level], gram[level])
        if size > 1:
            if level > 1:
                sum_chunks(level)
            plan[0]()
        shared_wait(level, 6)
        if level > 1 and size > 1:
            other_cross(level)
            run_all(sum_plan(level, 1, cross_part[level], cross[level]))
        right = rest[level][:, 0].reshape(wide, stripe).astype(jnp.float32)
        after = geometry[level - 1][0]
        at = lax.rem(c, after)
        if level > 1:
            right = (right - cross[level][0]).astype(jnp.bfloat16)
            tops[level - 1][at] = own_rows(level, right, all_tops[level])
            share(level - 1, 0, tops[level - 1].at[at])
        else:
            right = jnp.where(lax.rem(c, size) == 0, right, 0.0) - cross[1][0]
            parts[at] = right.astype(jnp.bfloat16)
            share(0, 0, parts.at[at])
        later = functools.partial(close, level, plan[1:])

    for block in (0, 1):
        each(1, cube, lambda d, block=block: route(d, block).wait_send())
    each(1, cube, lambda d: tell(d).wait_send())
    for low, high, copy in pending:
        for d in range(low, high):
            copy(d).wait_send()


def finish(width, total, pick, root, leaf, middle, upper, core_out, root_out, *refs):
    results, (work, low_factor, sems) = refs[:3], refs[3:]
    copies = [
        pltpu.make_async_copy(source, result, sems.at[k])
        for k, (source, result) in enumerate(zip((leaf, middle, upper), results))
    ]
    for copy in copies:
        copy.start()
    chosen = pick[...]
    wide, slots = chosen.shape
    low_factor[...] = jnp.zeros(low_factor.shape, jnp.float32)
    for k, (upper_part, _, below) in enumerate(factor_panels(total[...], width, work)):
        low = k * width
        low_factor[low : low + width, low : low + width] = mm32(eye(width), upper_part, NT)
        if below is not None:
            low_factor[low + width :, low : low + width] = below
    spread = mm32(low_factor[...], chosen, NN)
    narrow = chosen.astype(jnp.bfloat16)
    used = mm(narrow, jnp.ones((wide, slots), jnp.bfloat16), TN)
    core_out[...] = mm32(chosen, spread, TN) + eye(slots) * (1.0 - used)
    root_out[...] = mm(narrow, root[...], TN).astype(jnp.bfloat16)
    for copy in copies:
        copy.wait()


def body(
    cube,
    panel,
    columns,
    leaf_of,
    inverse_root,
    inverse_upper,
    inverse_middle,
    inverse_leaf,
    coupling_upper,
    coupling_middle,
    coupling_leaf,
):
    time_cols, _, stripe = columns.shape
    leaves = min(8, cube)
    leaf_share = cube // leaves
    per_slot = max(1, (2 * time_cols // leaves + leaf_share - 1) // leaf_share)
    width = cube * per_slot
    inverses = [inverse_leaf, inverse_middle, inverse_upper, inverse_root]
    couplings = [
        jnp.transpose(coupling_leaf, (1, 0, 2)),
        coupling_middle,
        jnp.transpose(coupling_upper, (1, 0, 2)),
    ]
    geometry = {}
    for level, inverse in zip(LEVELS, inverses):
        rows = inverse.shape[0]
        geometry[level] = (cube // min(2**level, cube), rows, rows // panel)
    wide = {level: geometry[level][0] * width for level in LEVELS}
    ranks = cube * time_cols
    slots = wide[0]
    wide[0] = ranks
    part = {level: geometry[level][2] for level in LEVELS}
    size = {level: geometry[level][0] for level in LEVELS}
    vm = pltpu.VMEM
    scratch = [vm(x.shape, x.dtype) for x in inverses]
    scratch += [vm(x.shape, x.dtype) for x in couplings]
    scratch += [vm((cube, 4, SLOT, stripe), jnp.bfloat16)] * 2
    scratch += [vm((8, 128), jnp.int32), vm((cube, 8, 128), jnp.int32)]
    scratch += [vm((size[l], width, stripe), jnp.bfloat16) for l in LEVELS[:3]]
    scratch += [vm((cube, wide[1], stripe), jnp.bfloat16)]
    scratch += [vm((size[l], l, width, stripe), jnp.bfloat16) for l in LEVELS[:3]]
    scratch += [vm((size[l], width, wide[l + 1]), jnp.float32) for l in LEVELS[1:]]
    scratch += [vm((size[l], width, wide[l]), jnp.float32) for l in LEVELS[:3]]
    scratch += [vm((size[l], width, stripe), jnp.bfloat16) for l in LEVELS[:3]]
    for _ in range(4):
        scratch += [vm((panel // 2, wide[l], part[l]), jnp.bfloat16) for l in LEVELS]
    scratch += [vm((panel // 2, 2, wide[l], part[l]), jnp.bfloat16) for l in LEVELS]
    scratch += [vm((wide[l], wide[l]), jnp.float32) for l in LEVELS]
    for l in LEVELS:
        steps = radices(size[l]) or [1]
        kind = jnp.float32 if size[l] <= 2 else jnp.bfloat16
        scratch += [vm((len(steps), max(steps), wide[l], wide[l]) if size[l] > 1 else (1, 1, 8, 128), kind)]
    scratch += [vm((l, wide[l], stripe), jnp.float32) for l in LEVELS[:3]]
    for l in LEVELS[:3]:
        steps = radices(size[l]) or [1]
        used = l > 1 and size[l] > 1
        scratch += [vm((len(steps), max(steps), l, wide[l], stripe) if used else (1, 1, 1, 16, 128), jnp.bfloat16)]
    scratch += [vm((width, 128), jnp.float32)]
    dma = pltpu.SemaphoreType.DMA
    scratch += [dma((4, 4)), dma((2, cube)), dma((2, cube)), dma((cube,)), dma((cube,)), dma((4, 4, panel // 2)), dma((4, 4, panel // 2))]
    scratch += [dma((4, 7, cube)), dma((4, 7, cube))]
    shape = jax.ShapeDtypeStruct
    passed = [shape((wide[l], part[l]), jnp.bfloat16) for l in LEVELS]
    outs = [shape((ranks, ranks), jnp.float32), shape((ranks, slots), jnp.float32)] + passed
    in_vmem = pl.BlockSpec(memory_space=pltpu.VMEM)
    in_any = pl.BlockSpec(memory_space=pl.ANY)
    total, pick, leaf, middle, upper, root = pl.pallas_call(
        functools.partial(kernel, cube, panel, width, per_slot, leaves, geometry),
        out_shape=outs,
        in_specs=[in_vmem, in_vmem] + [in_any] * 7,
        out_specs=[in_vmem] * 6,
        scratch_shapes=scratch,
        compiler_params=pltpu.CompilerParams(
            collective_id=0, has_side_effects=True, vmem_limit_bytes=58 * 2**20
        ),
    )(
        jnp.transpose(leaf_of),
        columns,
        *inverses,
        *couplings,
    )
    core, root, leaf, middle, upper = pl.pallas_call(
        functools.partial(finish, width),
        out_shape=[shape((slots, slots), jnp.float32), shape((slots, part[0]), jnp.bfloat16)]
        + passed[:3],
        in_specs=[in_vmem] * 6,
        out_specs=[in_vmem] * 2 + [in_any] * 3,
        scratch_shapes=[vm((width, 128), jnp.float32), vm((ranks, ranks), jnp.float32), dma((3,))],
    )(total, pick, root, leaf, middle, upper)
    return (core, root.T, upper.T, middle.T, leaf.T)


def solution(mesh):
    in_specs = (
        P("cube", None, "panel"),
        P("cube", None),
        P("cube", "panel"),
        P("cube", "panel"),
        P("cube", "panel"),
        P("cube", "panel"),
        P("cube", None, "panel"),
        P("cube", None, "panel"),
        P("cube", None, "panel"),
    )
    out_specs = (
        P(),
        P(("cube", "panel"), None),
        P(("cube", "panel"), None),
        P(("cube", "panel"), None),
        P(("cube", "panel"), None),
    )
    run = functools.partial(body, mesh.shape["cube"], mesh.shape["panel"])
    return jax.shard_map(run, mesh=mesh, in_specs=in_specs, out_specs=out_specs, check_vma=False)
```
